256 devices in a mesh: box: 16 (over x_lo, y, core), samp: 16 (over z, x_hi).
Axes of the slice: x: 4 (x_hi: 2, x_lo: 2; x = x_hi * 2 + x_lo), y: 4, z: 8, core: 2. Of those that a mesh axis runs over, the one named last changes fastest.
Arguments:
- xvec: bfloat16 [4096, 2, 4, 128], P(('box', 'samp')), may hold values from -6 to 6
- near_blocks: bfloat16 [4096, 8, 2, 128, 128], P(('box', 'samp')), may hold values from -0.1875 to 0.1875
- neighbours: int32 [4096, 8], P(('box', 'samp')), may hold values from 0 to 4095, as said below
- lift: bfloat16 [4096, 2, 128, 128], P(('box', 'samp')), may hold values from -0.5 to 0.5
- place: bfloat16 [4096, 2, 128, 128], P(('box', 'samp')), may hold values from -0.25 to 0.25
- interp: bfloat16 [2048, 128], replicated, may hold values from -0.5 to 0.5
- phases: float32 [8, 2, 2048], replicated, may hold values from -1 to 1, as said below
- octant: int32 [4096], P(('box', 'samp')), may hold values from 0 to 7, as said below
- leaf_parent_index: int32 [4096], P(('box', 'samp')), may hold values from 0 to 511, as said below
- translators: float32 [64, 2, 2048], P(None, None, 'samp'), may hold values from -0.5 to 0.5
- inter_list: int32 [512, 16], P('box'), may hold values from 0 to 511, as said below
- trans_id: int32 [512, 16], P('box'), may hold values from 0 to 63
Outputs:
- product: float32 [4096, 2, 4, 128], P(('box', 'samp'))
The draws below stay inside these ranges and needn't reach their ends.
Inputs may be any that keep to these rules, and one draw needn't show every extreme that they name: `neighbours`: row n starts with n itself; its other entries are distinct and lie within 8 boxes of n in cyclic order over all 4096 leaf boxes (the texture is periodic). `leaf_parent_index`: leaf box n belongs to box group g = n // 256 and its parent is one of that group's upper-level boxes g * 32 to g * 32 + 31; every upper-level box has exactly 8 children. `octant`: the 8 children of an upper-level box have 8 distinct octants. `inter_list`: entries of row p are distinct, each equal to p + d modulo 512 with 2 <= |d| <= 32 (the periodic tree's interaction zone). `phases`: each entry has magnitude one: real part squared plus imaginary part squared is 1.
All inputs are finite; a program needn't handle non-finite values.
Results may differ from the reference program's by a relative error of at most 0.0065.
Values may be sent and summed in bfloat16 or wider, within the bound.
A program may use at most 64 MiB of HBM per device.

```python
import math
import jax
import jax.numpy as jnp
from jax import lax

B_DEV = 16
U = 128
R = 4
K = 8
Q0 = 128
Q1 = 2048
NT = 64
NB = 4096
HB = 8
GB = 256
NPG = 32
NP = 512
KI = 16
N_BOX = 16


def draw_neighbours(key, part):
    offsets = jnp.concatenate([jnp.arange(-HB, 0, dtype=jnp.int32), jnp.arange(1, HB + 1, dtype=jnp.int32)])
    scores = jax.random.randint(key, (NB, 2 * HB), 0, 1 << 20) * (2 * HB) + jnp.arange(2 * HB, dtype=jnp.int32)[None, :]
    order = jnp.argsort(scores, axis=1)[:, :K - 1]
    picked = offsets[order]
    picked = jnp.concatenate([jnp.zeros((NB, 1), jnp.int32), picked], axis=1)
    return jnp.mod(jnp.arange(NB, dtype=jnp.int32)[:, None] + picked, NB).astype(jnp.int32)


def tree_slots(key):
    inner = jax.random.fold_in(key, 7)
    groups = NB // GB
    scores = jax.random.randint(inner, (groups, GB), 0, 1 << 20) * GB + jnp.arange(GB, dtype=jnp.int32)[None, :]
    return jnp.argsort(scores, axis=1).astype(jnp.int32)


def draw_leaf_parent_index(key, part):
    slots = tree_slots(key)
    groups = NB // GB
    base = jnp.arange(groups, dtype=jnp.int32)[:, None] * NPG
    return (base + slots // 8).reshape(NB).astype(jnp.int32)


def draw_octant(key, part):
    slots = tree_slots(key)
    return (slots % 8).reshape(NB).astype(jnp.int32)


def draw_phases(key, part):
    angle = jax.random.uniform(key, (8, Q1), jnp.float32, -math.pi, math.pi)
    return jnp.stack([jnp.cos(angle), jnp.sin(angle)], 1).astype(jnp.float32)


def draw_inter_list(key, part):
    reach = jnp.arange(2, NPG + 1, dtype=jnp.int32)
    offsets = jnp.concatenate([-reach, reach])
    width = 2 * NPG - 2
    scores = jax.random.randint(key, (NP, width), 0, 1 << 20) * width + jnp.arange(width, dtype=jnp.int32)[None, :]
    picked = offsets[jnp.argsort(scores, axis=1)[:, :KI]]
    return jnp.mod(jnp.arange(NP, dtype=jnp.int32)[:, None] + picked, NP).astype(jnp.int32)


def place_ends(drawn, stream_key, least, high):
    longest = drawn.shape.index(max(drawn.shape))
    spots = []
    for shift in (0, 1):
        where = [jax.random.randint(jax.random.fold_in(stream_key, axis), (), 0, length) for axis, length in enumerate(drawn.shape)]
        where[longest] = (where[longest] + shift) % drawn.shape[longest]
        spots.append(tuple(where))
    return drawn.at[spots[0]].set(least).at[spots[1]].set(high)


def steps_of(rng, dims, split, smallest, high):
    gain = 1.0
    for position, blocks in split:
        heights = jax.random.uniform(jax.random.fold_in(jax.random.fold_in(rng, 6), position), (blocks,), jnp.float32, smallest / len(split), high / len(split))
        gain = gain * jnp.repeat(jnp.exp(heights), dims[position] // blocks).reshape((-1,) + (1,) * (len(dims) - 1 - position))
    return gain


def noise(own_key, extent, scale, most, pieces=(), held_as=jnp.bfloat16):
    entries = jax.random.normal(own_key, extent, jnp.float32) * scale
    if len(pieces) > 0:
        entries = steps_of(own_key, extent, pieces, -0.22, 0.18) * entries
    return jnp.clip(entries, min=-most, max=most).astype(held_as)


def setup_inputs(seed: int = 0) -> dict:
    splits = jax.random.split(jax.random.key(seed), 13)
    return {
        "xvec": noise(splits[0], (NB, 2, R, U), 1.0, 6.0, ((0, 256),)),
        "near_blocks": noise(splits[1], (NB, K, 2, U, U), (K * U) ** -0.5, 0.1875, ((0, 256),)),
        "neighbours": draw_neighbours(jax.random.fold_in(splits[12], 71), 0),
        "lift": noise(splits[3], (NB, 2, Q0, U), U ** -0.5, 0.5, ((0, 256),)),
        "place": noise(splits[4], (NB, 2, U, Q0), (4 * Q0) ** -0.5, 0.25, ((0, 256),)),
        "interp": noise(splits[5], (Q1, Q0), Q0 ** -0.5, 0.5),
        "phases": draw_phases(jax.random.fold_in(splits[12], 71), 0),
        "octant": draw_octant(jax.random.fold_in(splits[12], 71), 0),
        "leaf_parent_index": draw_leaf_parent_index(jax.random.fold_in(splits[12], 71), 0),
        "translators": noise(splits[9], (NT, 2, Q1), (8 * KI) ** -0.5, 0.5, ((2, 16),), jnp.float32),
        "inter_list": draw_inter_list(jax.random.fold_in(splits[12], 71), 0),
        "trans_id": place_ends(jax.random.randint(splits[11], (NP, KI), 0, NT), jax.random.fold_in(splits[11], 1), 0, NT - 1).astype(jnp.int32),
    }


def cmul(ar, ai, br, bi):
    return ar * br - ai * bi, ar * bi + ai * br


def reference(xvec, near_blocks, neighbours, lift, place, interp, phases, octant, leaf_parent_index, translators, inter_list, trans_id):
    f32 = jnp.float32
    bf16 = jnp.bfloat16
    spans = NB // B_DEV

    def near_span(args):
        blocks, index, lifts, xs = args
        xn = xvec[index].astype(f32)
        z = blocks.astype(f32)

        def apply(a, b):
            return jnp.einsum('bkpq,bkrq->brp', a, b)

        yr = apply(z[:, :, 0], xn[:, :, 0]) - apply(z[:, :, 1], xn[:, :, 1])
        yi = apply(z[:, :, 0], xn[:, :, 1]) + apply(z[:, :, 1], xn[:, :, 0])
        lf = lifts.astype(f32)
        xf = xs.astype(f32)

        def radiate(a, b):
            return jnp.einsum('bqu,bru->brq', a, b)

        pr = radiate(lf[:, 0], xf[:, 0]) - radiate(lf[:, 1], xf[:, 1])
        pim = radiate(lf[:, 0], xf[:, 1]) + radiate(lf[:, 1], xf[:, 0])
        return jnp.stack([yr, yi], 1), jnp.stack([pr, pim], 1).astype(bf16)

    near, pattern = lax.map(near_span, (near_blocks.reshape(spans, B_DEV, K, 2, U, U), neighbours.reshape(spans, B_DEV, K), lift.reshape(spans, B_DEV, 2, Q0, U), xvec.reshape(spans, B_DEV, 2, R, U)))
    near = near.reshape(NB, 2, R, U)
    pattern = lax.optimization_barrier(pattern.reshape(NB, 2, R, Q0))
    interpolation_filter = interp.astype(f32)

    def up_group(args):
        group, pats, octs, pars = args
        upv = jnp.einsum('sq,bcrq->bcrs', interpolation_filter, pats.astype(f32))
        ph = phases[octs]
        cr, ci = cmul(ph[:, 0][:, None, :], ph[:, 1][:, None, :], upv[:, 0], upv[:, 1])
        indicator_matrix = (pars[None, :] == group * NPG + jnp.arange(NPG, dtype=jnp.int32)[:, None]).astype(f32)
        return jnp.stack([jnp.einsum('pb,brs->prs', indicator_matrix, cr), jnp.einsum('pb,brs->prs', indicator_matrix, ci)], 1)

    parents = lax.map(up_group, (jnp.arange(N_BOX, dtype=jnp.int32), pattern.reshape(N_BOX, GB, 2, R, Q0), octant.reshape(N_BOX, GB), leaf_parent_index.reshape(N_BOX, GB)))
    parents = lax.optimization_barrier(parents.reshape(NP, 2, R, Q1).astype(bf16))

    def translate(args):
        ilist, tids = args
        src = parents[ilist].astype(f32)
        tr = translators[tids]
        ar, ai = cmul(tr[:, :, 0][:, :, None, :], tr[:, :, 1][:, :, None, :], src[:, :, 0], src[:, :, 1])
        return jnp.stack([ar.sum(1), ai.sum(1)], 1)

    incoming = lax.map(translate, (inter_list.reshape(N_BOX, NPG, KI), trans_id.reshape(N_BOX, NPG, KI)))
    incoming = lax.optimization_barrier(incoming.reshape(NP, 2, R, Q1).astype(bf16))

    def down_group(args):
        octs, pars = args
        sel = incoming[pars].astype(f32)
        ph = phases[octs]
        sr, si = cmul(ph[:, 0][:, None, :], ph[:, 1][:, None, :], sel[:, 0], sel[:, 1])
        shifted = lax.optimization_barrier(jnp.stack([sr, si], 1).astype(bf16)).astype(f32)
        return jnp.einsum('bcrs,sq->bcrq', shifted, interpolation_filter).astype(bf16)

    field = lax.map(down_group, (octant.reshape(N_BOX, GB), leaf_parent_index.reshape(N_BOX, GB)))
    field = lax.optimization_barrier(field.reshape(NB, 2, R, Q0)).astype(f32)
    pl = place.astype(f32)

    def receive(a, b):
        return jnp.einsum('buq,brq->bru', a, b)

    fr = receive(pl[:, 0], field[:, 0]) - receive(pl[:, 1], field[:, 1])
    fi = receive(pl[:, 0], field[:, 1]) + receive(pl[:, 1], field[:, 0])
    return near + jnp.stack([fr, fi], 1)
```

```python
import jax
import jax.numpy as jnp
from jax import lax
from jax.experimental import pallas as pl
from jax.experimental.pallas import tpu as pltpu
from jax.sharding import PartitionSpec as P

f32 = jnp.float32
bf16 = jnp.bfloat16
MESH = pl.DeviceIdType.MESH
NT_DIMS = (((1,), (1,)), ((), ()))


def dot_nt(a, b):
    return lax.dot_general(a, b, NT_DIMS, preferred_element_type=f32)


def dot_nn(a, b):
    return jnp.dot(a, b, preferred_element_type=f32)


def times_i(v):
    swapped = pltpu.roll(v, 4, 0)
    row = lax.broadcasted_iota(jnp.int32, v.shape, 0)
    return jnp.where(row < 4, -swapped, swapped)


def make_kernel(nbox, nsamp, boxes, parents, near_k, list_k, sample_share):
    half = boxes // 2
    total_boxes = boxes * nsamp * nbox
    total_parents = parents * nbox
    blk = boxes * 8
    pb = parents * 8
    slots = boxes * nsamp
    share = sample_share

    def kernel(
        nbr, octs, pars, ilist, tids,
        x_hbm, near_hbm, lift_hbm, place_hbm, interp_hbm, phases_hbm, trans_hbm,
        out,
        xh, xf, nearm, liftm, placem, interpm, phm, trm,
        patf, slotf, gbuf, parf, parw, parb, hbuf, incf, sbuf, rbuf, nearf, fieldf,
        near_sem, in_sem,
        halo_send, halo_recv, g_send, g_recv, h_send, h_recv, a_send, a_recv,
    ):
        b = lax.axis_index("box")
        s = lax.axis_index("samp")
        me = b * nsamp + s
        ndev = nbox * nsamp

        x_cp = pltpu.make_async_copy(x_hbm, xh.at[pl.ds(half * 8, blk)], in_sem.at[0])
        lift_cp = pltpu.make_async_copy(lift_hbm, liftm, in_sem.at[1])
        interp_cp = pltpu.make_async_copy(interp_hbm, interpm, in_sem.at[2])
        ph_cp = pltpu.make_async_copy(
            phases_hbm.at[:, :, pl.ds(pl.multiple_of(s * share, share), share)], phm, in_sem.at[3]
        )
        tr_cp = pltpu.make_async_copy(trans_hbm, trm, in_sem.at[4])
        place_cp = pltpu.make_async_copy(place_hbm, placem, in_sem.at[5])
        near_cps = [
            pltpu.make_async_copy(near_hbm.at[n], nearm.at[n], near_sem.at[n]) for n in range(boxes)
        ]
        x_cp.start()
        lift_cp.start()

        barrier = pltpu.get_barrier_semaphore()
        right = lax.rem(me + 1, ndev)
        left = lax.rem(me + ndev - 1, ndev)
        right_id = (right // nsamp, lax.rem(right, nsamp))
        left_id = (left // nsamp, lax.rem(left, nsamp))
        up_id = (lax.rem(b + 1, nbox), s)
        down_id = (lax.rem(b + nbox - 1, nbox), s)

        def peer(t):
            return (b, lax.rem(s + t + nsamp, nsamp))

        for dev in (right_id, left_id, up_id, down_id):
            pl.semaphore_signal(barrier, inc=1, device_id=dev, device_id_type=MESH)
        for t in range(1, nsamp):
            pl.semaphore_signal(barrier, inc=1, device_id=peer(t), device_id_type=MESH)

        interp_cp.start()
        ph_cp.start()
        tr_cp.start()
        for cp in near_cps[: boxes // 2]:
            cp.start()
        place_cp.start()
        for cp in near_cps[boxes // 2 :]:
            cp.start()

        for n in range(boxes):
            slot = octs[n] * parents + (pars[n] - b * parents)
            slotf[pl.ds(n, 1), :] = jnp.full((1, 128), slot, jnp.int32).astype(f32)
        x_cp.wait()
        xf[pl.ds(half, boxes)] = xh[pl.ds(half * 8, blk), :].astype(f32).reshape(boxes, 8, 128)
        lift_cp.wait()

        for n in range(boxes):
            xn = xf[half + n].astype(bf16)
            o = dot_nt(xn, liftm[n].reshape(2 * liftm.shape[2], liftm.shape[3]))
            patf[pl.ds(n, 8, stride=boxes), :] = o[:, :128] + times_i(o[:, 128:])
        gbuf[0, pl.ds(0, blk), :] = patf[...].astype(bf16)
        gbuf[0, pl.ds(blk, boxes), :] = slotf[...].astype(bf16)

        pl.semaphore_wait(barrier, nsamp - 1 + 4)

        to_right = pltpu.make_async_remote_copy(
            src_ref=xh.at[pl.ds(blk, half * 8)], dst_ref=xh.at[pl.ds(0, half * 8)],
            send_sem=halo_send.at[0], recv_sem=halo_recv.at[0],
            device_id=right_id, device_id_type=MESH,
        )
        to_left = pltpu.make_async_remote_copy(
            src_ref=xh.at[pl.ds(half * 8, half * 8)], dst_ref=xh.at[pl.ds(blk + half * 8, half * 8)],
            send_sem=halo_send.at[1], recv_sem=halo_recv.at[1],
            device_id=left_id, device_id_type=MESH,
        )
        to_right.start()
        to_left.start()
        order = sorted(range(1, nsamp), key=lambda t: -min(t, nsamp - t))
        gathers = {
            t: pltpu.make_async_remote_copy(
                src_ref=gbuf.at[0], dst_ref=gbuf.at[t],
                send_sem=g_send.at[t], recv_sem=g_recv.at[t],
                device_id=peer(t), device_id_type=MESH,
            )
            for t in range(1, nsamp)
        }
        for t in order:
            gathers[t].start()

        to_right.wait()
        to_left.wait()
        xf[pl.ds(0, half)] = xh[pl.ds(0, half * 8), :].astype(f32).reshape(half, 8, 128)
        xf[pl.ds(half + boxes, half)] = (
            xh[pl.ds(blk + half * 8, half * 8), :].astype(f32).reshape(half, 8, 128)
        )

        def near_box(n, carry):
            pltpu.make_async_copy(near_hbm.at[n], nearm.at[n], near_sem.at[n]).wait()
            acc = jnp.zeros((8, 256), f32)
            for k in range(near_k):
                idx = lax.rem(nbr[n, k] - me * boxes + half + total_boxes, 2 * boxes)
                xk = xf[idx].astype(bf16)
                acc = acc + dot_nt(xk, nearm[n, k].reshape(256, 128))
            nearf[pl.ds(pl.multiple_of(n * 8, 8), 8), :] = acc[:, :128] + times_i(acc[:, 128:])
            return carry

        lax.fori_loop(0, boxes // 2, near_box, 0)

        interp_cp.wait()
        ph_cp.wait()
        tr_cp.wait()
        for t in range(1, nsamp):
            gathers[t].wait()

        ids = gbuf[:, pl.ds(blk, boxes), :].reshape(slots, 128).astype(f32)
        lane = lax.broadcasted_iota(jnp.int32, (slots, 128), 1).astype(f32)
        spread = jnp.concatenate(
            [jnp.where(ids == lane + 128.0 * h, 1.0, 0.0) for h in range(slots // 128)], axis=1
        ).astype(bf16)
        ids_t = ids.T
        row = lax.broadcasted_iota(jnp.int32, (128, slots), 0).astype(f32)
        gather_m = jnp.concatenate(
            [jnp.where(ids_t == row + 128.0 * h, 1.0, 0.0) for h in range(slots // 128)], axis=0
        ).astype(bf16)
        interp_own = interpm[pl.ds(pl.multiple_of(s * share, share), share), :]

        def raised(cr):
            sorted_pat = dot_nn(
                gather_m, gbuf[:, pl.ds(cr * boxes, boxes), :].reshape(slots, 128)
            ).astype(bf16)
            return dot_nt(sorted_pat, interp_own)

        for r in range(4):
            ar, ai = raised(r), raised(4 + r)
            pr = jnp.zeros((parents, 128), f32)
            pi = jnp.zeros((parents, 128), f32)
            for o in range(8):
                fr, fi = phm[o, pl.ds(0, 1), :], phm[o, pl.ds(1, 1), :]
                br, bi = ar[o * parents : (o + 1) * parents], ai[o * parents : (o + 1) * parents]
                pr = pr + (fr * br - fi * bi)
                pi = pi + (fr * bi + fi * br)
            parf[pl.ds(r, parents, stride=8), :] = pr
            parf[pl.ds(4 + r, parents, stride=8), :] = pi
        parb[...] = parf[...].astype(bf16)

        to_up = pltpu.make_async_remote_copy(
            src_ref=parb, dst_ref=hbuf.at[0], send_sem=h_send.at[0], recv_sem=h_recv.at[0],
            device_id=up_id, device_id_type=MESH,
        )
        to_down = pltpu.make_async_remote_copy(
            src_ref=parb, dst_ref=hbuf.at[1], send_sem=h_send.at[1], recv_sem=h_recv.at[1],
            device_id=down_id, device_id_type=MESH,
        )
        to_up.start()
        to_down.start()
        parw[pl.ds(parents, parents)] = parb[...].astype(f32).reshape(parents, 8, 128)
        to_up.wait()
        parw[pl.ds(0, parents)] = hbuf[0].astype(f32).reshape(parents, 8, 128)
        to_down.wait()
        parw[pl.ds(2 * parents, parents)] = hbuf[1].astype(f32).reshape(parents, 8, 128)

        def translate(p, carry):
            s1 = jnp.zeros((8, 128), f32)
            s2 = jnp.zeros((8, 128), f32)
            for k in range(list_k):
                w = lax.rem(ilist[p, k] - b * parents + parents + total_parents, total_parents)
                v = parw[jnp.minimum(w, 3 * parents - 1)]
                op = trm[tids[p, k]]
                s1 = s1 + op[0:1] * v
                s2 = s2 + op[1:2] * v
            inc = (s1 + times_i(s2)).astype(bf16).astype(f32)
            incf[pl.ds(pl.multiple_of(p * 8, 8), 8), :] = inc
            return carry

        lax.fori_loop(0, parents, translate, 0)

        for r in range(4):
            ir = incf[pl.ds(r, parents, stride=8), :]
            ii = incf[pl.ds(4 + r, parents, stride=8), :]
            sr, si = [], []
            for o in range(8):
                fr, fi = phm[o, pl.ds(0, 1), :], phm[o, pl.ds(1, 1), :]
                sr.append((fr * ir - fi * ii).astype(bf16))
                si.append((fr * ii + fi * ir).astype(bf16))
            for cr, part in ((r, sr), (4 + r, si)):
                u = dot_nn(spread, jnp.concatenate(part, axis=0)).astype(bf16)
                sbuf[:, pl.ds(cr * boxes, boxes), :] = u.reshape(nsamp, boxes, 128)

        sends = {
            t: pltpu.make_async_remote_copy(
                src_ref=sbuf.at[t], dst_ref=rbuf.at[t],
                send_sem=a_send.at[t], recv_sem=a_recv.at[t],
                device_id=peer(-t), device_id_type=MESH,
            )
            for t in range(1, nsamp)
        }
        for t in order:
            sends[t].start()

        lax.fori_loop(boxes // 2, boxes, near_box, 0)

        def lowered(t, block):
            j = lax.rem(s + t, nsamp)
            return dot_nn(block, interpm[pl.ds(pl.multiple_of(j * share, share), share), :])

        field = lowered(0, sbuf[0])
        for t in sorted(range(1, nsamp), key=lambda t: min(t, nsamp - t)):
            sends[t].wait()
            field = field + lowered(t, rbuf[t])
        fieldf[...] = field
        place_cp.wait()
        for n in range(boxes):
            fn = fieldf[pl.ds(n, 8, stride=boxes), :].astype(bf16)
            o = dot_nt(fn, placem[n].reshape(256, 128))
            out[pl.ds(n * 8, 8), :] = nearf[pl.ds(n * 8, 8), :] + o[:, :128] + times_i(o[:, 128:])

    return kernel


def on_device(
    xvec, near_blocks, neighbours, lift, place, interp, phases, octant,
    leaf_parent_index, translators, inter_list, trans_id,
):
    boxes = xvec.shape[0]
    nsamp = lax.axis_size("samp")
    nbox = lax.axis_size("box")
    parents = inter_list.shape[0]
    share = interp.shape[0] // nsamp
    blk = boxes * 8
    x2 = xvec.reshape(blk, 128)
    smem = pl.BlockSpec(memory_space=pltpu.SMEM)
    hbm = pl.BlockSpec(memory_space=pltpu.HBM)
    dma = pltpu.SemaphoreType.DMA
    out = pl.pallas_call(
        make_kernel(nbox, nsamp, boxes, parents, neighbours.shape[1], inter_list.shape[1], share),
        out_shape=jax.ShapeDtypeStruct((blk, 128), f32),
        in_specs=[smem] * 5 + [hbm] * 7,
        out_specs=pl.BlockSpec(memory_space=pltpu.VMEM),
        scratch_shapes=[
            pltpu.VMEM((2 * blk, 128), bf16),
            pltpu.VMEM((2 * boxes, 8, 128), f32),
            pltpu.VMEM(near_blocks.shape, bf16),
            pltpu.VMEM(lift.shape, bf16),
            pltpu.VMEM(place.shape, bf16),
            pltpu.VMEM(interp.shape, bf16),
            pltpu.VMEM((8, 2, share), f32),
            pltpu.VMEM(translators.shape, f32),
            pltpu.VMEM((blk, 128), f32),
            pltpu.VMEM((boxes, 128), f32),
            pltpu.VMEM((nsamp, blk + boxes, 128), bf16),
            pltpu.VMEM((parents * 8, 128), f32),
            pltpu.VMEM((3 * parents, 8, 128), f32),
            pltpu.VMEM((parents * 8, 128), bf16),
            pltpu.VMEM((2, parents * 8, 128), bf16),
            pltpu.VMEM((parents * 8, 128), f32),
            pltpu.VMEM((nsamp, blk, 128), bf16),
            pltpu.VMEM((nsamp, blk, 128), bf16),
            pltpu.VMEM((blk, 128), f32),
            pltpu.VMEM((blk, 128), f32),
            dma((boxes,)),
            dma((6,)),
            dma((2,)), dma((2,)),
            dma((nsamp,)), dma((nsamp,)),
            dma((2,)), dma((2,)),
            dma((nsamp,)), dma((nsamp,)),
        ],
        compiler_params=pltpu.CompilerParams(
            collective_id=0, has_side_effects=True, vmem_limit_bytes=60 * 1024 * 1024
        ),
    )(
        neighbours, octant, leaf_parent_index, inter_list, trans_id,
        x2, near_blocks, lift, place, interp, phases, translators,
    )
    return out.reshape(xvec.shape)


def solution(mesh):
    lead = ("box", "samp")
    in_specs = (
        P(lead, None, None, None),
        P(lead, None, None, None, None),
        P(lead, None),
        P(lead, None, None, None),
        P(lead, None, None, None),
        P(),
        P(),
        P(lead),
        P(lead),
        P(None, None, "samp"),
        P("box", None),
        P("box", None),
    )
    return jax.shard_map(
        on_device, mesh=mesh, in_specs=in_specs, out_specs=P(lead, None, None, None), check_vma=False
    )
```

```python
import jax
import jax.numpy as jnp
from jax import lax
from jax.experimental import pallas as pl
from jax.experimental.pallas import tpu as pltpu
from jax.sharding import PartitionSpec as P

f32 = jnp.float32
bf16 = jnp.bfloat16
MESH = pl.DeviceIdType.MESH
NT_DIMS = (((1,), (1,)), ((), ()))


def dot_nt(a, b):
    return lax.dot_general(a, b, NT_DIMS, preferred_element_type=f32)


def dot_nn(a, b):
    return jnp.dot(a, b, preferred_element_type=f32)


def times_i(v):
    swapped = pltpu.roll(v, 4, 0)
    row = lax.broadcasted_iota(jnp.int32, v.shape, 0)
    return jnp.where(row < 4, -swapped, swapped)


def make_kernel(nbox, nsamp, boxes, parents, near_k, list_k, sample_share):
    half = boxes // 2
    total_boxes = boxes * nsamp * nbox
    total_parents = parents * nbox
    blk = boxes * 8
    pb = parents * 8
    slots = boxes * nsamp
    nz = nsamp // 2
    share = sample_share

    def kernel(
        nbr, octs, pars, ilist, tids,
        x_hbm, near_hbm, lift_hbm, place_hbm, interp_hbm, phases_hbm, trans_hbm,
        out,
        xh, xf, nearm, liftm, placem, interpm, phm, trm, trb,
        patf, slotf, gbuf, parf, parw, parb, hbuf, incf,
        ownf, xsend, xrecv, zsend, zrecv, nearf, fieldf,
        near_sem, in_sem,
        halo_send, halo_recv, g_send, g_recv, h_send, h_recv,
        ax_send, ax_recv, az_send, az_recv,
    ):
        b = lax.axis_index("box")
        s = lax.axis_index("samp")
        me = b * nsamp + s
        ndev = nbox * nsamp

        x_cp = pltpu.make_async_copy(x_hbm, xh.at[pl.ds(half * 8, blk)], in_sem.at[0])
        lift_cp = pltpu.make_async_copy(lift_hbm, liftm, in_sem.at[1])
        interp_cp = pltpu.make_async_copy(
            interp_hbm.at[pl.ds(pl.multiple_of(s * share, share), share)], interpm, in_sem.at[2]
        )
        ph_cp = pltpu.make_async_copy(
            phases_hbm.at[:, :, pl.ds(pl.multiple_of(s * share, share), share)], phm, in_sem.at[3]
        )
        tr_cp = pltpu.make_async_copy(trans_hbm, trm, in_sem.at[4])
        place_cp = pltpu.make_async_copy(place_hbm, placem, in_sem.at[5])
        near_cps = [
            pltpu.make_async_copy(near_hbm.at[n], nearm.at[n], near_sem.at[n]) for n in range(boxes)
        ]
        x_cp.start()
        lift_cp.start()

        barrier = pltpu.get_barrier_semaphore()
        right = lax.rem(me + 1, ndev)
        left = lax.rem(me + ndev - 1, ndev)
        right_id = (right // nsamp, lax.rem(right, nsamp))
        left_id = (left // nsamp, lax.rem(left, nsamp))
        up_id = (lax.rem(b + 1, nbox), s)
        down_id = (lax.rem(b + nbox - 1, nbox), s)

        z, xhi = s // 2, lax.rem(s, 2)
        partner = (b, s + 1 - 2 * xhi)

        def along(t):
            return (b, 2 * lax.rem(z + t + nz, nz) + xhi)

        for dev in (right_id, left_id, up_id, down_id, partner):
            pl.semaphore_signal(barrier, inc=1, device_id=dev, device_id_type=MESH)
        for t in range(1, nz):
            pl.semaphore_signal(barrier, inc=1, device_id=along(t), device_id_type=MESH)

        interp_cp.start()
        ph_cp.start()
        tr_cp.start()
        for cp in near_cps[: boxes // 2]:
            cp.start()
        place_cp.start()
        for cp in near_cps[boxes // 2 :]:
            cp.start()

        for n in range(boxes):
            slot = octs[n] * parents + (pars[n] - b * parents)
            slotf[pl.ds(n, 1), :] = jnp.full((1, 128), slot, jnp.int32).astype(f32)
        x_cp.wait()
        xf[pl.ds(half, boxes)] = xh[pl.ds(half * 8, blk), :].astype(f32).reshape(boxes, 8, 128)
        lift_cp.wait()

        for n in range(boxes):
            xn = xf[half + n].astype(bf16)
            o = dot_nt(xn, liftm[n].reshape(2 * liftm.shape[2], liftm.shape[3]))
            patf[pl.ds(n, 8, stride=boxes), :] = o[:, :128] + times_i(o[:, 128:])
        gbuf[0, pl.ds(0, blk), :] = patf[...].astype(bf16)
        gbuf[0, pl.ds(blk, boxes), :] = slotf[...].astype(bf16)

        pl.semaphore_wait(barrier, nz - 1 + 5)

        to_right = pltpu.make_async_remote_copy(
            src_ref=xh.at[pl.ds(blk, half * 8)], dst_ref=xh.at[pl.ds(0, half * 8)],
            send_sem=halo_send.at[0], recv_sem=halo_recv.at[0],
            device_id=right_id, device_id_type=MESH,
        )
        to_left = pltpu.make_async_remote_copy(
            src_ref=xh.at[pl.ds(half * 8, half * 8)], dst_ref=xh.at[pl.ds(blk + half * 8, half * 8)],
            send_sem=halo_send.at[1], recv_sem=halo_recv.at[1],
            device_id=left_id, device_id_type=MESH,
        )
        to_right.start()
        to_left.start()
        order = sorted(range(1, nz), key=lambda t: -min(t, nz - t))

        def spread_out(t):
            return pltpu.make_async_remote_copy(
                src_ref=gbuf.at[0], dst_ref=gbuf.at[t],
                send_sem=g_send.at[t], recv_sem=g_recv.at[t],
                device_id=along(t), device_id_type=MESH,
            )

        def hand_over(t):
            return pltpu.make_async_remote_copy(
                src_ref=gbuf.at[t], dst_ref=gbuf.at[nz + t],
                send_sem=g_send.at[nz + t], recv_sem=g_recv.at[nz + t],
                device_id=partner, device_id_type=MESH,
            )

        gathers = {t: spread_out(t) for t in order}
        gathers.update({nz + t: hand_over(t) for t in range(nz)})
        for t in order:
            gathers[t].start()
        gathers[nz].start()

        to_right.wait()
        to_left.wait()
        xf[pl.ds(0, half)] = xh[pl.ds(0, half * 8), :].astype(f32).reshape(half, 8, 128)
        xf[pl.ds(half + boxes, half)] = (
            xh[pl.ds(blk + half * 8, half * 8), :].astype(f32).reshape(half, 8, 128)
        )

        def near_box(n, carry):
            pltpu.make_async_copy(near_hbm.at[n], nearm.at[n], near_sem.at[n]).wait()
            acc = jnp.zeros((8, 256), f32)
            for k in range(near_k):
                idx = lax.rem(nbr[k, n] - me * boxes + half + total_boxes, 2 * boxes)
                xk = xf[idx].astype(bf16)
                acc = acc + dot_nt(xk, nearm[n, k].reshape(256, 128))
            nearf[pl.ds(pl.multiple_of(n * 8, 8), 8), :] = acc[:, :128] + times_i(acc[:, 128:])
            return carry

        done = 0
        for i, t in enumerate(order):
            upto = boxes * (i + 1) // (2 * len(order))
            lax.fori_loop(done, upto, near_box, 0)
            done = upto
            gathers[t].wait_recv()
            gathers[nz + t].start()

        interp_cp.wait()
        ph_cp.wait()
        tr_cp.wait()

        def widen(t, carry):
            op = trm[t]
            trb[2 * t] = jnp.broadcast_to(op[0:1], (8, 128))
            trb[2 * t + 1] = jnp.broadcast_to(op[1:2], (8, 128))
            return carry

        lax.fori_loop(0, trm.shape[0], widen, 0, unroll=8)
        for t in order:
            gathers[t].wait_send()
        for t in range(nz):
            gathers[nz + t].wait()

        ids = gbuf[:, pl.ds(blk, boxes), :].reshape(slots, 128).astype(f32)
        lane = lax.broadcasted_iota(jnp.int32, (slots, 128), 1).astype(f32)
        spread = jnp.concatenate(
            [jnp.where(ids == lane + 128.0 * h, 1.0, 0.0) for h in range(slots // 128)], axis=1
        ).astype(bf16)
        ids_t = ids.T
        row = lax.broadcasted_iota(jnp.int32, (128, slots), 0).astype(f32)
        gather_m = jnp.concatenate(
            [jnp.where(ids_t == row + 128.0 * h, 1.0, 0.0) for h in range(slots // 128)], axis=0
        ).astype(bf16)
        interp_own = interpm[...]

        def raised(cr):
            sorted_pat = dot_nn(
                gather_m, gbuf[:, pl.ds(cr * boxes, boxes), :].reshape(slots, 128)
            ).astype(bf16)
            return dot_nt(sorted_pat, interp_own)

        halos = {
            (side, r): pltpu.make_async_remote_copy(
                src_ref=parb.at[r], dst_ref=hbuf.at[side, r],
                send_sem=h_send.at[side, r], recv_sem=h_recv.at[side, r],
                device_id=(up_id, down_id)[side], device_id_type=MESH,
            )
            for side in range(2)
            for r in range(4)
        }
        for r in range(4):
            ar, ai = raised(r), raised(4 + r)
            pr = jnp.zeros((parents, 128), f32)
            pi = jnp.zeros((parents, 128), f32)
            for o in range(8):
                fr, fi = phm[o, pl.ds(0, 1), :], phm[o, pl.ds(1, 1), :]
                br, bi = ar[o * parents : (o + 1) * parents], ai[o * parents : (o + 1) * parents]
                pr = pr + (fr * br - fi * bi)
                pi = pi + (fr * bi + fi * br)
            parb[r, 0] = pr.astype(bf16)
            parb[r, 1] = pi.astype(bf16)
            for side in range(2):
                halos[side, r].start()

        def keep(block, src):
            for r in range(4):
                for c in range(2):
                    parf[pl.ds(block * pb + 4 * c + r, parents, stride=8), :] = src(r, c).astype(f32)
            parw[pl.ds(block * parents, parents)] = parf[pl.ds(block * pb, pb), :].reshape(parents, 8, 128)

        keep(1, lambda r, c: parb[r, c])
        for side in range(2):
            for r in range(4):
                halos[side, r].wait()
            keep(2 * side, lambda r, c: hbuf[side, r, c])

        def translate(p, carry):
            s1 = jnp.zeros((8, 128), f32)
            s2 = jnp.zeros((8, 128), f32)
            for k in range(list_k):
                w = lax.rem(ilist[k, p] - b * parents + parents + total_parents, total_parents)
                v = parw[jnp.minimum(w, 3 * parents - 1)]
                t = 2 * tids[k, p]
                s1 = s1 + trb[t] * v
                s2 = s2 + trb[t + 1] * v
            inc = (s1 + times_i(s2)).astype(bf16).astype(f32)
            incf[pl.ds(pl.multiple_of(p * 8, 8), 8), :] = inc
            return carry

        lax.fori_loop(0, parents, translate, 0)

        to_partner = [
            pltpu.make_async_remote_copy(
                src_ref=xsend.at[t], dst_ref=xrecv.at[t],
                send_sem=ax_send.at[t], recv_sem=ax_recv.at[t],
                device_id=partner, device_id_type=MESH,
            )
            for t in range(nz)
        ]
        to_owner = {
            t: pltpu.make_async_remote_copy(
                src_ref=zsend.at[t], dst_ref=zrecv.at[t],
                send_sem=az_send.at[t], recv_sem=az_recv.at[t],
                device_id=along(-t), device_id_type=MESH,
            )
            for t in range(1, nz)
        }
        rows = slots // 2
        for r in range(4):
            ir = incf[pl.ds(r, parents, stride=8), :]
            ii = incf[pl.ds(4 + r, parents, stride=8), :]
            sr, si = [], []
            for o in range(8):
                fr, fi = phm[o, pl.ds(0, 1), :], phm[o, pl.ds(1, 1), :]
                sr.append((fr * ir - fi * ii).astype(bf16))
                si.append((fr * ii + fi * ir).astype(bf16))
            for cr, part in ((r, sr), (4 + r, si)):
                u = dot_nn(spread, jnp.concatenate(part, axis=0)).astype(bf16)
                low = dot_nn(u, interp_own)
                ownf[:, pl.ds(cr * boxes, boxes), :] = low[:rows].reshape(nz, boxes, 128)
                xsend[:, pl.ds(cr * boxes, boxes), :] = low[rows:].astype(bf16).reshape(nz, boxes, 128)
        for t in order:
            to_partner[t].start()
        to_partner[0].start()
        done = boxes // 2
        for i, t in enumerate(order):
            to_partner[t].wait_recv()
            zsend[t] = (ownf[t] + xrecv[t].astype(f32)).astype(bf16)
            to_owner[t].start()
            upto = boxes // 2 + boxes * (i + 1) // (2 * len(order))
            lax.fori_loop(done, upto, near_box, 0)
            done = upto
        to_partner[0].wait_recv()
        field = ownf[0] + xrecv[0].astype(f32)
        for t in range(nz):
            to_partner[t].wait_send()
        for t in order[::-1]:
            to_owner[t].wait()
            field = field + zrecv[t].astype(f32)
        fieldf[...] = field
        place_cp.wait()
        for n in range(boxes):
            fn = fieldf[pl.ds(n, 8, stride=boxes), :].astype(bf16)
            o = dot_nt(fn, placem[n].reshape(256, 128))
            out[pl.ds(n * 8, 8), :] = nearf[pl.ds(n * 8, 8), :] + o[:, :128] + times_i(o[:, 128:])

    return kernel


def on_device(
    xvec, near_blocks, neighbours, lift, place, interp, phases, octant,
    leaf_parent_index, translators, inter_list, trans_id,
):
    boxes = xvec.shape[0]
    nsamp = lax.axis_size("samp")
    nbox = lax.axis_size("box")
    parents = inter_list.shape[0]
    share = interp.shape[0] // nsamp
    blk = boxes * 8
    nz = nsamp // 2
    x2 = xvec.reshape(blk, 128)
    smem = pl.BlockSpec(memory_space=pltpu.SMEM)
    hbm = pl.BlockSpec(memory_space=pltpu.HBM)
    dma = pltpu.SemaphoreType.DMA
    out = pl.pallas_call(
        make_kernel(nbox, nsamp, boxes, parents, neighbours.shape[1], inter_list.shape[1], share),
        out_shape=jax.ShapeDtypeStruct((blk, 128), f32),
        in_specs=[smem] * 5 + [hbm] * 7,
        out_specs=pl.BlockSpec(memory_space=pltpu.VMEM),
        scratch_shapes=[
            pltpu.VMEM((2 * blk, 128), bf16),
            pltpu.VMEM((2 * boxes, 8, 128), f32),
            pltpu.VMEM(near_blocks.shape, bf16),
            pltpu.VMEM(lift.shape, bf16),
            pltpu.VMEM(place.shape, bf16),
            pltpu.VMEM((share, interp.shape[1]), bf16),
            pltpu.VMEM((8, 2, share), f32),
            pltpu.VMEM(translators.shape, f32),
            pltpu.VMEM((2 * translators.shape[0], 8, 128), f32),
            pltpu.VMEM((blk, 128), f32),
            pltpu.VMEM((boxes, 128), f32),
            pltpu.VMEM((nsamp, blk + boxes, 128), bf16),
            pltpu.VMEM((3 * parents * 8, 128), f32),
            pltpu.VMEM((3 * parents, 8, 128), f32),
            pltpu.VMEM((4, 2, parents, 128), bf16),
            pltpu.VMEM((2, 4, 2, parents, 128), bf16),
            pltpu.VMEM((parents * 8, 128), f32),
            pltpu.VMEM((nz, blk, 128), f32),
            pltpu.VMEM((nz, blk, 128), bf16),
            pltpu.VMEM((nz, blk, 128), bf16),
            pltpu.VMEM((nz, blk, 128), bf16),
            pltpu.VMEM((nz, blk, 128), bf16),
            pltpu.VMEM((blk, 128), f32),
            pltpu.VMEM((blk, 128), f32),
            dma((boxes,)),
            dma((6,)),
            dma((2,)), dma((2,)),
            dma((nsamp,)), dma((nsamp,)),
            dma((2, 4)), dma((2, 4)),
            dma((nz,)), dma((nz,)),
            dma((nz,)), dma((nz,)),
        ],
        compiler_params=pltpu.CompilerParams(
            collective_id=0, has_side_effects=True, vmem_limit_bytes=60 * 1024 * 1024
        ),
    )(
        neighbours.T, octant, leaf_parent_index, inter_list.T, trans_id.T,
        x2, near_blocks, lift, place, interp, phases, translators,
    )
    return out.reshape(xvec.shape)


def solution(mesh):
    lead = ("box", "samp")
    in_specs = (
        P(lead, None, None, None),
        P(lead, None, None, None, None),
        P(lead, None),
        P(lead, None, None, None),
        P(lead, None, None, None),
        P(),
        P(),
        P(lead),
        P(lead),
        P(None, None, "samp"),
        P("box", None),
        P("box", None),
    )
    return jax.shard_map(
        on_device, mesh=mesh, in_specs=in_specs, out_specs=P(lead, None, None, None), check_vma=False
    )
```

```python
import jax
import jax.numpy as jnp
from jax import lax
from jax.experimental import pallas as pl
from jax.experimental.pallas import tpu as pltpu
from jax.sharding import PartitionSpec as P

f32 = jnp.float32
bf16 = jnp.bfloat16
MESH = pl.DeviceIdType.MESH
NT_DIMS = (((1,), (1,)), ((), ()))


def dot_nt(a, b):
    return lax.dot_general(a, b, NT_DIMS, preferred_element_type=f32)


def dot_nn(a, b):
    return jnp.dot(a, b, preferred_element_type=f32)


def times_i(v):
    swapped = pltpu.roll(v, 4, 0)
    row = lax.broadcasted_iota(jnp.int32, v.shape, 0)
    return jnp.where(row < 4, -swapped, swapped)


def make_kernel(nbox, nsamp, boxes, parents, near_k, list_k, sample_share):
    half = boxes // 2
    total_boxes = boxes * nsamp * nbox
    total_parents = parents * nbox
    blk = boxes * 8
    pb = parents * 8
    slots = boxes * nsamp
    nz = nsamp // 2
    half_rows = blk // 2
    share = sample_share

    def kernel(
        nbr_hbm, octs_hbm, pars_hbm, ilist_hbm, tids_hbm,
        x_hbm, near_hbm, lift_hbm, place_hbm, interp_hbm, phases_hbm, trans_hbm,
        out,
        nbr, octs, pars, ilist, tids, wtab,
        xh, xf, nearm, liftm, placem, interpm, phm, trm, trb,
        patf, slotf, gbuf, parf, parw, parb, hbuf, incf,
        ownf, xsend, xrecv, zsend, zrecv, nearf, fieldf,
        near_sem, in_sem, idx_sem,
        halo_send, halo_recv, g_send, g_recv, h_send, h_recv,
        ax_send, ax_recv, az_send, az_recv,
    ):
        b = lax.axis_index("box")
        s = lax.axis_index("samp")
        me = b * nsamp + s
        ndev = nbox * nsamp

        x_cp = pltpu.make_async_copy(x_hbm, xh.at[pl.ds(half * 8, blk)], in_sem.at[0])
        lift_cp = pltpu.make_async_copy(lift_hbm, liftm, in_sem.at[1])
        interp_cp = pltpu.make_async_copy(
            interp_hbm.at[pl.ds(pl.multiple_of(s * share, share), share)], interpm, in_sem.at[2]
        )
        ph_cp = pltpu.make_async_copy(
            phases_hbm.at[:, :, pl.ds(pl.multiple_of(s * share, share), share)], phm, in_sem.at[3]
        )
        tr_cp = pltpu.make_async_copy(trans_hbm, trm, in_sem.at[4])
        place_cp = pltpu.make_async_copy(place_hbm, placem, in_sem.at[5])
        near_cps = [
            pltpu.make_async_copy(near_hbm.at[n], nearm.at[n], near_sem.at[n]) for n in range(boxes)
        ]
        idx_cps = [
            pltpu.make_async_copy(src, dst, idx_sem.at[i])
            for i, (src, dst) in enumerate(
                ((octs_hbm, octs), (pars_hbm, pars), (nbr_hbm, nbr), (ilist_hbm, ilist), (tids_hbm, tids))
            )
        ]
        x_cp.start()
        lift_cp.start()
        for cp in idx_cps:
            cp.start()

        barrier = pltpu.get_barrier_semaphore()
        right = lax.rem(me + 1, ndev)
        left = lax.rem(me + ndev - 1, ndev)
        right_id = (right // nsamp, lax.rem(right, nsamp))
        left_id = (left // nsamp, lax.rem(left, nsamp))
        up_id = (lax.rem(b + 1, nbox), s)
        down_id = (lax.rem(b + nbox - 1, nbox), s)

        z, xhi = s // 2, lax.rem(s, 2)
        partner = (b, s + 1 - 2 * xhi)

        def along(t):
            return (b, 2 * lax.rem(z + t + nz, nz) + xhi)

        for dev in (right_id, left_id, up_id, down_id, partner):
            pl.semaphore_signal(barrier, inc=1, device_id=dev, device_id_type=MESH)
        for t in range(1, nz):
            pl.semaphore_signal(barrier, inc=1, device_id=along(t), device_id_type=MESH)

        interp_cp.start()
        ph_cp.start()
        tr_cp.start()
        for cp in near_cps[: boxes // 2]:
            cp.start()
        place_cp.start()
        for cp in near_cps[boxes // 2 :]:
            cp.start()

        idx_cps[0].wait()
        idx_cps[1].wait()
        for n in range(boxes):
            slot = octs[n] * parents + (pars[n] - b * parents)
            slotf[pl.ds(n, 1), :] = jnp.full((1, 128), slot, jnp.int32).astype(f32)
        x_cp.wait()
        xf[pl.ds(half, boxes)] = xh[pl.ds(half * 8, blk), :].astype(f32).reshape(boxes, 8, 128)
        lift_cp.wait()

        for n in range(boxes):
            xn = xf[half + n].astype(bf16)
            o = dot_nt(xn, liftm[n].reshape(2 * liftm.shape[2], liftm.shape[3]))
            patf[pl.ds(n, 8, stride=boxes), :] = o[:, :128] + times_i(o[:, 128:])
        gbuf[0, pl.ds(0, blk), :] = patf[...].astype(bf16)
        gbuf[0, pl.ds(blk, boxes), :] = slotf[...].astype(bf16)

        pl.semaphore_wait(barrier, nz - 1 + 5)

        to_right = pltpu.make_async_remote_copy(
            src_ref=xh.at[pl.ds(blk, half * 8)], dst_ref=xh.at[pl.ds(0, half * 8)],
            send_sem=halo_send.at[0], recv_sem=halo_recv.at[0],
            device_id=right_id, device_id_type=MESH,
        )
        to_left = pltpu.make_async_remote_copy(
            src_ref=xh.at[pl.ds(half * 8, half * 8)], dst_ref=xh.at[pl.ds(blk + half * 8, half * 8)],
            send_sem=halo_send.at[1], recv_sem=halo_recv.at[1],
            device_id=left_id, device_id_type=MESH,
        )
        to_right.start()
        to_left.start()
        order = sorted(range(1, nz), key=lambda t: -min(t, nz - t))

        def spread_out(t):
            return pltpu.make_async_remote_copy(
                src_ref=gbuf.at[0], dst_ref=gbuf.at[t],
                send_sem=g_send.at[t], recv_sem=g_recv.at[t],
                device_id=along(t), device_id_type=MESH,
            )

        def hand_over(t):
            return pltpu.make_async_remote_copy(
                src_ref=gbuf.at[t], dst_ref=gbuf.at[nz + t],
                send_sem=g_send.at[nz + t], recv_sem=g_recv.at[nz + t],
                device_id=partner, device_id_type=MESH,
            )

        gathers = {t: spread_out(t) for t in order}
        gathers.update({nz + t: hand_over(t) for t in range(nz)})
        for t in order:
            gathers[t].start()
        gathers[nz].start()

        for cp in idx_cps[2:]:
            cp.wait()

        def window(p, carry):
            for k in range(list_k):
                w = lax.rem(ilist[k, p] - b * parents + parents + total_parents, total_parents)
                wtab[k, p] = jnp.minimum(w, 3 * parents - 1)
            return carry

        lax.fori_loop(0, parents, window, 0)
        to_right.wait()
        to_left.wait()
        xf[pl.ds(0, half)] = xh[pl.ds(0, half * 8), :].astype(f32).reshape(half, 8, 128)
        xf[pl.ds(half + boxes, half)] = (
            xh[pl.ds(blk + half * 8, half * 8), :].astype(f32).reshape(half, 8, 128)
        )

        def near_box(n, carry):
            pltpu.make_async_copy(near_hbm.at[n], nearm.at[n], near_sem.at[n]).wait()
            acc = jnp.zeros((8, 256), f32)
            for k in range(near_k):
                idx = lax.rem(nbr[k, n] - me * boxes + half + total_boxes, 2 * boxes)
                xk = xf[idx].astype(bf16)
                acc = acc + dot_nt(xk, nearm[n, k].reshape(256, 128))
            nearf[pl.ds(pl.multiple_of(n * 8, 8), 8), :] = acc[:, :128] + times_i(acc[:, 128:])
            return carry

        done = 0
        for i, t in enumerate(order):
            upto = boxes * (i + 1) // (2 * len(order))
            lax.fori_loop(done, upto, near_box, 0)
            done = upto
            gathers[t].wait_recv()
            gathers[nz + t].start()

        interp_cp.wait()
        ph_cp.wait()
        tr_cp.wait()

        def widen(t, carry):
            op = trm[t]
            trb[2 * t] = jnp.broadcast_to(op[0:1], (8, 128))
            trb[2 * t + 1] = jnp.broadcast_to(op[1:2], (8, 128))
            return carry

        lax.fori_loop(0, trm.shape[0], widen, 0, unroll=8)
        for t in order:
            gathers[t].wait_send()
        for t in range(nz):
            gathers[nz + t].wait()

        ids = gbuf[:, pl.ds(blk, boxes), :].reshape(slots, 128).astype(f32)
        lane = lax.broadcasted_iota(jnp.int32, (slots, 128), 1).astype(f32)
        spread = jnp.concatenate(
            [jnp.where(ids == lane + 128.0 * h, 1.0, 0.0) for h in range(slots // 128)], axis=1
        ).astype(bf16)
        ids_t = ids.T
        row = lax.broadcasted_iota(jnp.int32, (128, slots), 0).astype(f32)
        gather_m = jnp.concatenate(
            [jnp.where(ids_t == row + 128.0 * h, 1.0, 0.0) for h in range(slots // 128)], axis=0
        ).astype(bf16)
        interp_own = interpm[...]

        def raised(cr):
            sorted_pat = dot_nn(
                gather_m, gbuf[:, pl.ds(cr * boxes, boxes), :].reshape(slots, 128)
            ).astype(bf16)
            return dot_nt(sorted_pat, interp_own)

        halos = {
            (side, r): pltpu.make_async_remote_copy(
                src_ref=parb.at[r], dst_ref=hbuf.at[side, r],
                send_sem=h_send.at[side, r], recv_sem=h_recv.at[side, r],
                device_id=(up_id, down_id)[side], device_id_type=MESH,
            )
            for side in range(2)
            for r in range(4)
        }
        for r in range(4):
            ar, ai = raised(r), raised(4 + r)
            pr = jnp.zeros((parents, 128), f32)
            pi = jnp.zeros((parents, 128), f32)
            for o in range(8):
                fr, fi = phm[o, pl.ds(0, 1), :], phm[o, pl.ds(1, 1), :]
                br, bi = ar[o * parents : (o + 1) * parents], ai[o * parents : (o + 1) * parents]
                pr = pr + (fr * br - fi * bi)
                pi = pi + (fr * bi + fi * br)
            parb[r, 0] = pr.astype(bf16)
            parb[r, 1] = pi.astype(bf16)
            for side in range(2):
                halos[side, r].start()

        def keep(block, src):
            for r in range(4):
                for c in range(2):
                    parf[pl.ds(block * pb + 4 * c + r, parents, stride=8), :] = src(r, c).astype(f32)
            parw[pl.ds(block * parents, parents)] = parf[pl.ds(block * pb, pb), :].reshape(parents, 8, 128)

        keep(1, lambda r, c: parb[r, c])
        for side in range(2):
            for r in range(4):
                halos[side, r].wait()
            keep(2 * side, lambda r, c: hbuf[side, r, c])

        def translate(p, carry):
            s1 = jnp.zeros((8, 128), f32)
            s2 = jnp.zeros((8, 128), f32)
            for k in range(list_k):
                v = parw[wtab[k, p]]
                t = 2 * tids[k, p]
                s1 = s1 + trb[t] * v
                s2 = s2 + trb[t + 1] * v
            inc = (s1 + times_i(s2)).astype(bf16).astype(f32)
            incf[pl.ds(pl.multiple_of(p * 8, 8), 8), :] = inc
            return carry

        lax.fori_loop(0, parents, translate, 0, unroll=4)

        to_partner = {
            (t, h): pltpu.make_async_remote_copy(
                src_ref=xsend.at[t, pl.ds(h * half_rows, half_rows)],
                dst_ref=xrecv.at[t, pl.ds(h * half_rows, half_rows)],
                send_sem=ax_send.at[t, h], recv_sem=ax_recv.at[t, h],
                device_id=partner, device_id_type=MESH,
            )
            for t in range(nz)
            for h in range(2)
        }
        to_owner = {
            t: pltpu.make_async_remote_copy(
                src_ref=zsend.at[t], dst_ref=zrecv.at[t],
                send_sem=az_send.at[t], recv_sem=az_recv.at[t],
                device_id=along(-t), device_id_type=MESH,
            )
            for t in range(1, nz)
        }
        rows = slots // 2
        turn = order + [0]
        for r in range(4):
            ir = incf[pl.ds(r, parents, stride=8), :]
            ii = incf[pl.ds(4 + r, parents, stride=8), :]
            sr, si = [], []
            for o in range(8):
                fr, fi = phm[o, pl.ds(0, 1), :], phm[o, pl.ds(1, 1), :]
                sr.append((fr * ir - fi * ii).astype(bf16))
                si.append((fr * ii + fi * ir).astype(bf16))
            for cr, part in ((2 * r, sr), (2 * r + 1, si)):
                u = dot_nn(spread, jnp.concatenate(part, axis=0)).astype(bf16)
                low = dot_nn(u, interp_own)
                ownf[:, pl.ds(cr * boxes, boxes), :] = low[:rows].reshape(nz, boxes, 128)
                xsend[:, pl.ds(cr * boxes, boxes), :] = low[rows:].astype(bf16).reshape(nz, boxes, 128)
            if r % 2 == 1:
                for t in turn:
                    to_partner[t, r // 2].start()
        done = boxes // 2
        for i, t in enumerate(order):
            for h in range(2):
                to_partner[t, h].wait_recv()
            zsend[t] = (ownf[t] + xrecv[t].astype(f32)).astype(bf16)
            to_owner[t].start()
            upto = boxes // 2 + boxes * (i + 1) // (2 * len(order))
            lax.fori_loop(done, upto, near_box, 0)
            done = upto
        for h in range(2):
            to_partner[0, h].wait_recv()
        field = ownf[0] + xrecv[0].astype(f32)
        for t in range(nz):
            for h in range(2):
                to_partner[t, h].wait_send()
        for t in order[::-1]:
            to_owner[t].wait()
            field = field + zrecv[t].astype(f32)
        for r in range(4):
            for c in range(2):
                fieldf[pl.ds((4 * c + r) * boxes, boxes), :] = (
                    field[(2 * r + c) * boxes : (2 * r + c + 1) * boxes]
                )
        place_cp.wait()
        for n in range(boxes):
            fn = fieldf[pl.ds(n, 8, stride=boxes), :].astype(bf16)
            o = dot_nt(fn, placem[n].reshape(256, 128))
            out[pl.ds(n * 8, 8), :] = nearf[pl.ds(n * 8, 8), :] + o[:, :128] + times_i(o[:, 128:])

    return kernel


def on_device(
    xvec, near_blocks, neighbours, lift, place, interp, phases, octant,
    leaf_parent_index, translators, inter_list, trans_id,
):
    boxes = xvec.shape[0]
    nsamp = lax.axis_size("samp")
    nbox = lax.axis_size("box")
    parents = inter_list.shape[0]
    share = interp.shape[0] // nsamp
    blk = boxes * 8
    nz = nsamp // 2
    x2 = xvec.reshape(blk, 128)
    hbm = pl.BlockSpec(memory_space=pltpu.HBM)
    dma = pltpu.SemaphoreType.DMA
    out = pl.pallas_call(
        make_kernel(nbox, nsamp, boxes, parents, neighbours.shape[1], inter_list.shape[1], share),
        out_shape=jax.ShapeDtypeStruct((blk, 128), f32),
        in_specs=[hbm] * 12,
        out_specs=pl.BlockSpec(memory_space=pltpu.VMEM),
        scratch_shapes=[
            pltpu.SMEM(neighbours.shape[::-1], jnp.int32),
            pltpu.SMEM(octant.shape, jnp.int32),
            pltpu.SMEM(octant.shape, jnp.int32),
            pltpu.SMEM(inter_list.shape[::-1], jnp.int32),
            pltpu.SMEM(inter_list.shape[::-1], jnp.int32),
            pltpu.SMEM(inter_list.shape[::-1], jnp.int32),
            pltpu.VMEM((2 * blk, 128), bf16),
            pltpu.VMEM((2 * boxes, 8, 128), f32),
            pltpu.VMEM(near_blocks.shape, bf16),
            pltpu.VMEM(lift.shape, bf16),
            pltpu.VMEM(place.shape, bf16),
            pltpu.VMEM((share, interp.shape[1]), bf16),
            pltpu.VMEM((8, 2, share), f32),
            pltpu.VMEM(translators.shape, f32),
            pltpu.VMEM((2 * translators.shape[0], 8, 128), f32),
            pltpu.VMEM((blk, 128), f32),
            pltpu.VMEM((boxes, 128), f32),
            pltpu.VMEM((nsamp, blk + boxes, 128), bf16),
            pltpu.VMEM((3 * parents * 8, 128), f32),
            pltpu.VMEM((3 * parents, 8, 128), f32),
            pltpu.VMEM((4, 2, parents, 128), bf16),
            pltpu.VMEM((2, 4, 2, parents, 128), bf16),
            pltpu.VMEM((parents * 8, 128), f32),
            pltpu.VMEM((nz, blk, 128), f32),
            pltpu.VMEM((nz, blk, 128), bf16),
            pltpu.VMEM((nz, blk, 128), bf16),
            pltpu.VMEM((nz, blk, 128), bf16),
            pltpu.VMEM((nz, blk, 128), bf16),
            pltpu.VMEM((blk, 128), f32),
            pltpu.VMEM((blk, 128), f32),
            dma((boxes,)),
            dma((6,)), dma((5,)),
            dma((2,)), dma((2,)),
            dma((nsamp,)), dma((nsamp,)),
            dma((2, 4)), dma((2, 4)),
            dma((nz, 2)), dma((nz, 2)),
            dma((nz,)), dma((nz,)),
        ],
        compiler_params=pltpu.CompilerParams(
            collective_id=0, has_side_effects=True, vmem_limit_bytes=48 * 1024 * 1024
        ),
    )(
        *[
            pltpu.with_memory_space_constraint(a, pltpu.HBM)
            for a in (
                neighbours.T, octant, leaf_parent_index, inter_list.T, trans_id.T,
                x2, near_blocks, lift, place, interp, phases, translators,
            )
        ]
    )
    return out.reshape(xvec.shape)


def solution(mesh):
    lead = ("box", "samp")
    in_specs = (
        P(lead, None, None, None),
        P(lead, None, None, None, None),
        P(lead, None),
        P(lead, None, None, None),
        P(lead, None, None, None),
        P(),
        P(),
        P(lead),
        P(lead),
        P(None, None, "samp"),
        P("box", None),
        P("box", None),
    )
    return jax.shard_map(
        on_device, mesh=mesh, in_specs=in_specs, out_specs=P(lead, None, None, None), check_vma=False
    )
```

```python
import jax
import jax.numpy as jnp
from jax import lax
from jax.experimental import pallas as pl
from jax.experimental.pallas import tpu as pltpu
from jax.sharding import PartitionSpec as P

f32 = jnp.float32
bf16 = jnp.bfloat16
MESH = pl.DeviceIdType.MESH
NT_DIMS = (((1,), (1,)), ((), ()))


def dot_nt(a, b):
    return lax.dot_general(a, b, NT_DIMS, preferred_element_type=f32)


def dot_nn(a, b):
    return jnp.dot(a, b, preferred_element_type=f32)


def times_i(v):
    swapped = pltpu.roll(v, 4, 0)
    row = lax.broadcasted_iota(jnp.int32, v.shape, 0)
    return jnp.where(row < 4, -swapped, swapped)


def make_kernel(nbox, nsamp, boxes, parents, near_k, list_k, sample_share):
    half = boxes // 2
    total_boxes = boxes * nsamp * nbox
    total_parents = parents * nbox
    blk = boxes * 8
    pb = parents * 8
    slots = boxes * nsamp
    nz = nsamp // 2
    half_rows = blk // 2
    relay_out = (7, 6, 1)
    relay_back = (1, 2, 7)
    share = sample_share

    def kernel(
        nbr_hbm, octs_hbm, pars_hbm, ilist_hbm, tids_hbm,
        x_hbm, near_hbm, lift_hbm, place_hbm, interp_hbm, phases_hbm, trans_hbm,
        out,
        nbr, octs, pars, ilist, tids, wtab,
        xh, xf, nearm, liftm, placem, interpm, twin, phm, trm, trb,
        patf, slotf, gbuf, parf, parw, parb, hbuf, incf,
        ownf, crossf, xsend, xrecv, brecv, zsend, zrecv, nearf, fieldf,
        near_sem, in_sem, idx_sem,
        halo_send, halo_recv, g_send, g_recv, h_send, h_recv,
        ax_send, ax_recv, b_send, b_recv, az_send, az_recv,
    ):
        b = lax.axis_index("box")
        s = lax.axis_index("samp")
        me = b * nsamp + s
        ndev = nbox * nsamp

        x_cp = pltpu.make_async_copy(x_hbm, xh.at[pl.ds(half * 8, blk)], in_sem.at[0])
        lift_cp = pltpu.make_async_copy(lift_hbm, liftm, in_sem.at[1])
        interp_cp = pltpu.make_async_copy(
            interp_hbm.at[pl.ds(pl.multiple_of(s * share, share), share)], interpm, in_sem.at[2]
        )
        ph_cp = pltpu.make_async_copy(
            phases_hbm.at[:, :, pl.ds(pl.multiple_of(s * share, share), share)], phm, in_sem.at[3]
        )
        tr_cp = pltpu.make_async_copy(trans_hbm, trm, in_sem.at[4])
        place_cp = pltpu.make_async_copy(place_hbm, placem, in_sem.at[5])
        near_cps = [
            pltpu.make_async_copy(near_hbm.at[n], nearm.at[n], near_sem.at[n]) for n in range(boxes)
        ]
        idx_cps = [
            pltpu.make_async_copy(src, dst, idx_sem.at[i])
            for i, (src, dst) in enumerate(
                ((octs_hbm, octs), (pars_hbm, pars), (nbr_hbm, nbr), (ilist_hbm, ilist), (tids_hbm, tids))
            )
        ]
        x_cp.start()
        lift_cp.start()
        for cp in idx_cps:
            cp.start()

        barrier = pltpu.get_barrier_semaphore()
        right = lax.rem(me + 1, ndev)
        left = lax.rem(me + ndev - 1, ndev)
        right_id = (right // nsamp, lax.rem(right, nsamp))
        left_id = (left // nsamp, lax.rem(left, nsamp))
        up_id = (lax.rem(b + 1, nbox), s)
        down_id = (lax.rem(b + nbox - 1, nbox), s)

        z, xhi = s // 2, lax.rem(s, 2)
        partner = (b, s + 1 - 2 * xhi)

        def along(t):
            return (b, 2 * lax.rem(z + t + nz, nz) + xhi)

        for dev in (right_id, left_id, up_id, down_id, partner):
            pl.semaphore_signal(barrier, inc=1, device_id=dev, device_id_type=MESH)
        for t in range(1, nz):
            pl.semaphore_signal(barrier, inc=1, device_id=along(t), device_id_type=MESH)

        interp_cp.start()
        ph_cp.start()
        tr_cp.start()
        for cp in near_cps[: boxes // 2]:
            cp.start()
        place_cp.start()
        for cp in near_cps[boxes // 2 :]:
            cp.start()

        idx_cps[0].wait()
        idx_cps[1].wait()
        for n in range(boxes):
            slot = octs[n] * parents + (pars[n] - b * parents)
            slotf[pl.ds(n, 1), :] = jnp.full((1, 128), slot, jnp.int32).astype(f32)
        x_cp.wait()
        xf[pl.ds(half, boxes)] = xh[pl.ds(half * 8, blk), :].astype(f32).reshape(boxes, 8, 128)
        lift_cp.wait()

        for n in range(boxes):
            xn = xf[half + n].astype(bf16)
            o = dot_nt(xn, liftm[n].reshape(2 * liftm.shape[2], liftm.shape[3]))
            patf[pl.ds(n, 8, stride=boxes), :] = o[:, :128] + times_i(o[:, 128:])
        gbuf[0, pl.ds(0, blk), :] = patf[...].astype(bf16)
        gbuf[0, pl.ds(blk, boxes), :] = slotf[...].astype(bf16)

        pl.semaphore_wait(barrier, nz - 1 + 5)

        to_right = pltpu.make_async_remote_copy(
            src_ref=xh.at[pl.ds(blk, half * 8)], dst_ref=xh.at[pl.ds(0, half * 8)],
            send_sem=halo_send.at[0], recv_sem=halo_recv.at[0],
            device_id=right_id, device_id_type=MESH,
        )
        to_left = pltpu.make_async_remote_copy(
            src_ref=xh.at[pl.ds(half * 8, half * 8)], dst_ref=xh.at[pl.ds(blk + half * 8, half * 8)],
            send_sem=halo_send.at[1], recv_sem=halo_recv.at[1],
            device_id=left_id, device_id_type=MESH,
        )
        to_right.start()
        to_left.start()
        order = sorted(range(1, nz), key=lambda t: -min(t, nz - t))

        def spread_out(t):
            return pltpu.make_async_remote_copy(
                src_ref=gbuf.at[0], dst_ref=gbuf.at[t],
                send_sem=g_send.at[t], recv_sem=g_recv.at[t],
                device_id=along(t), device_id_type=MESH,
            )

        def hand_over(t):
            return pltpu.make_async_remote_copy(
                src_ref=gbuf.at[t], dst_ref=gbuf.at[nz + t],
                send_sem=g_send.at[nz + t], recv_sem=g_recv.at[nz + t],
                device_id=partner, device_id_type=MESH,
            )

        def pass_on(t):
            return pltpu.make_async_remote_copy(
                src_ref=gbuf.at[nz], dst_ref=gbuf.at[nz + t],
                send_sem=g_send.at[nz + t], recv_sem=g_recv.at[nz + t],
                device_id=along(t), device_id_type=MESH,
            )

        gathers = {t: spread_out(t) for t in order}
        gathers.update({nz + t: pass_on(t) if t in relay_out else hand_over(t) for t in range(nz)})
        gathers[nz].start()
        for t in order:
            gathers[t].start()

        for cp in idx_cps[2:]:
            cp.wait()

        def window(p, carry):
            for k in range(list_k):
                w = lax.rem(ilist[k, p] - b * parents + parents + total_parents, total_parents)
                wtab[k, p] = jnp.minimum(w, 3 * parents - 1)
            return carry

        lax.fori_loop(0, parents, window, 0)
        to_right.wait()
        to_left.wait()
        xf[pl.ds(0, half)] = xh[pl.ds(0, half * 8), :].astype(f32).reshape(half, 8, 128)
        xf[pl.ds(half + boxes, half)] = (
            xh[pl.ds(blk + half * 8, half * 8), :].astype(f32).reshape(half, 8, 128)
        )

        def near_box(n, carry):
            pltpu.make_async_copy(near_hbm.at[n], nearm.at[n], near_sem.at[n]).wait()
            acc = jnp.zeros((8, 256), f32)
            for k in range(near_k):
                idx = lax.rem(nbr[k, n] - me * boxes + half + total_boxes, 2 * boxes)
                xk = xf[idx].astype(bf16)
                acc = acc + dot_nt(xk, nearm[n, k].reshape(256, 128))
            nearf[pl.ds(pl.multiple_of(n * 8, 8), 8), :] = acc[:, :128] + times_i(acc[:, 128:])
            return carry

        lax.fori_loop(0, 3, near_box, 0)
        gathers[nz].wait_recv()
        for t in relay_out:
            gathers[nz + t].start()
        done = 3
        for i, t in enumerate(order):
            upto = 3 + (boxes // 2 - 3) * (i + 1) // len(order)
            lax.fori_loop(done, upto, near_box, 0)
            done = upto
            gathers[t].wait_recv()
            if t not in relay_out:
                gathers[nz + t].start()

        interp_cp.wait()
        twin[...] = jnp.zeros(twin.shape, bf16)
        twin[pl.ds(0, share), pl.ds(0, 128)] = interpm[...]
        twin[pl.ds(share, share), pl.ds(128, 128)] = interpm[...]
        ph_cp.wait()
        tr_cp.wait()

        def widen(t, carry):
            op = trm[t]
            trb[2 * t] = jnp.broadcast_to(op[0:1], (8, 128))
            trb[2 * t + 1] = jnp.broadcast_to(op[1:2], (8, 128))
            return carry

        lax.fori_loop(0, trm.shape[0], widen, 0, unroll=8)
        for t in order:
            gathers[t].wait_send()
        gathers[nz].wait_send()
        for t in order:
            gathers[nz + t].wait()

        ids = gbuf[:, pl.ds(blk, boxes), :].reshape(slots, 128).astype(f32)
        lane = lax.broadcasted_iota(jnp.int32, (slots, 128), 1).astype(f32)
        spread = jnp.concatenate(
            [jnp.where(ids == lane + 128.0 * h, 1.0, 0.0) for h in range(slots // 128)], axis=1
        ).astype(bf16)
        ids_t = ids.T
        row = lax.broadcasted_iota(jnp.int32, (128, slots), 0).astype(f32)
        gather_m = jnp.concatenate(
            [jnp.where(ids_t == row + 128.0 * h, 1.0, 0.0) for h in range(slots // 128)], axis=0
        ).astype(bf16)

        def raised(r):
            pair = jnp.concatenate(
                [
                    gbuf[:, pl.ds(cr * boxes, boxes), :].reshape(slots, 128)
                    for cr in (r, 4 + r)
                ],
                axis=1,
            )
            return dot_nt(dot_nn(gather_m, pair).astype(bf16), twin[...])

        halos = {
            (side, r): pltpu.make_async_remote_copy(
                src_ref=parb.at[r], dst_ref=hbuf.at[side, r],
                send_sem=h_send.at[side, r], recv_sem=h_recv.at[side, r],
                device_id=(up_id, down_id)[side], device_id_type=MESH,
            )
            for side in range(2)
            for r in range(4)
        }
        for r in range(4):
            both = raised(r)
            ar, ai = both[:, :128], both[:, 128:]
            pr = jnp.zeros((parents, 128), f32)
            pi = jnp.zeros((parents, 128), f32)
            for o in range(8):
                fr, fi = phm[o, pl.ds(0, 1), :], phm[o, pl.ds(1, 1), :]
                br, bi = ar[o * parents : (o + 1) * parents], ai[o * parents : (o + 1) * parents]
                pr = pr + (fr * br - fi * bi)
                pi = pi + (fr * bi + fi * br)
            parb[r, 0] = pr.astype(bf16)
            parb[r, 1] = pi.astype(bf16)
            for side in range(2):
                halos[side, r].start()

        def keep(block, src):
            for r in range(4):
                for c in range(2):
                    parf[pl.ds(block * pb + 4 * c + r, parents, stride=8), :] = src(r, c).astype(f32)
            parw[pl.ds(block * parents, parents)] = parf[pl.ds(block * pb, pb), :].reshape(parents, 8, 128)

        keep(1, lambda r, c: parb[r, c])
        for side in range(2):
            for r in range(4):
                halos[side, r].wait()
            keep(2 * side, lambda r, c: hbuf[side, r, c])

        def translate(p, carry):
            s1 = jnp.zeros((8, 128), f32)
            s2 = jnp.zeros((8, 128), f32)
            for k in range(list_k):
                v = parw[wtab[k, p]]
                t = 2 * tids[k, p]
                s1 = s1 + trb[t] * v
                s2 = s2 + trb[t + 1] * v
            inc = (s1 + times_i(s2)).astype(bf16).astype(f32)
            incf[pl.ds(pl.multiple_of(p * 8, 8), 8), :] = inc
            return carry

        lax.fori_loop(0, parents, translate, 0, unroll=4)

        turn = [t for t in order if t not in relay_back] + [0]
        to_partner = {
            (t, h): pltpu.make_async_remote_copy(
                src_ref=xsend.at[t, pl.ds(h * half_rows, half_rows)],
                dst_ref=xrecv.at[t, pl.ds(h * half_rows, half_rows)],
                send_sem=ax_send.at[t, h], recv_sem=ax_recv.at[t, h],
                device_id=partner, device_id_type=MESH,
            )
            for t in turn
            for h in range(2)
        }
        to_relay = {
            t: pltpu.make_async_remote_copy(
                src_ref=xsend.at[t], dst_ref=brecv.at[t],
                send_sem=b_send.at[t], recv_sem=b_recv.at[t],
                device_id=along(-t), device_id_type=MESH,
            )
            for t in relay_back
        }
        to_owner = {
            t: pltpu.make_async_remote_copy(
                src_ref=zsend.at[t], dst_ref=zrecv.at[t],
                send_sem=az_send.at[t], recv_sem=az_recv.at[t],
                device_id=along(-t), device_id_type=MESH,
            )
            for t in range(1, nz)
        }
        rows = slots // 2
        for r in range(4):
            ir = incf[pl.ds(r, parents, stride=8), :]
            ii = incf[pl.ds(4 + r, parents, stride=8), :]
            sr, si = [], []
            for o in range(8):
                fr, fi = phm[o, pl.ds(0, 1), :], phm[o, pl.ds(1, 1), :]
                sr.append((fr * ir - fi * ii).astype(bf16))
                si.append((fr * ii + fi * ir).astype(bf16))
            pair = jnp.concatenate([jnp.concatenate(sr, axis=0), jnp.concatenate(si, axis=0)], axis=1)
            both = dot_nn(dot_nn(spread, pair).astype(bf16), twin[...])
            for cr, low in ((2 * r, both[:, :128]), (2 * r + 1, both[:, 128:])):
                ownf[:, pl.ds(cr * boxes, boxes), :] = low[:rows].reshape(nz, boxes, 128)
                xsend[:, pl.ds(cr * boxes, boxes), :] = low[rows:].astype(bf16).reshape(nz, boxes, 128)
                crossf[pl.ds(cr * boxes, boxes), :] = low[rows : rows + boxes]
            if r % 2 == 1:
                for t in turn[:-1]:
                    to_partner[t, r // 2].start()
        for t in relay_back:
            to_relay[t].start()
        for t in relay_back:
            zsend[t] = ownf[t].astype(bf16)
            to_owner[t].start()

        def add_partner(t):
            for h in range(2):
                to_partner[t, h].wait_recv()
            zsend[t] = (ownf[t] + xrecv[t].astype(f32)).astype(bf16)
            to_owner[t].start()

        add_partner(turn[0])
        cross = crossf[...]
        for t in relay_back:
            to_relay[t].wait_recv()
            cross = cross + brecv[t].astype(f32)
        xsend[0] = cross.astype(bf16)
        for h in range(2):
            to_partner[0, h].start()
        for t in turn[1:-1]:
            add_partner(t)
        lax.fori_loop(boxes // 2, boxes, near_box, 0)
        for h in range(2):
            to_partner[0, h].wait_recv()
        field = ownf[0] + xrecv[0].astype(f32)
        for t in turn:
            for h in range(2):
                to_partner[t, h].wait_send()
        for t in relay_back:
            to_relay[t].wait_send()
        for t in order[::-1]:
            to_owner[t].wait()
            field = field + zrecv[t].astype(f32)
        for r in range(4):
            for c in range(2):
                fieldf[pl.ds((4 * c + r) * boxes, boxes), :] = (
                    field[(2 * r + c) * boxes : (2 * r + c + 1) * boxes]
                )
        place_cp.wait()
        for n in range(boxes):
            fn = fieldf[pl.ds(n, 8, stride=boxes), :].astype(bf16)
            o = dot_nt(fn, placem[n].reshape(256, 128))
            out[pl.ds(n * 8, 8), :] = nearf[pl.ds(n * 8, 8), :] + o[:, :128] + times_i(o[:, 128:])

    return kernel


def on_device(
    xvec, near_blocks, neighbours, lift, place, interp, phases, octant,
    leaf_parent_index, translators, inter_list, trans_id,
):
    boxes = xvec.shape[0]
    nsamp = lax.axis_size("samp")
    nbox = lax.axis_size("box")
    parents = inter_list.shape[0]
    share = interp.shape[0] // nsamp
    blk = boxes * 8
    nz = nsamp // 2
    x2 = xvec.reshape(blk, 128)
    hbm = pl.BlockSpec(memory_space=pltpu.HBM)
    dma = pltpu.SemaphoreType.DMA
    out = pl.pallas_call(
        make_kernel(nbox, nsamp, boxes, parents, neighbours.shape[1], inter_list.shape[1], share),
        out_shape=jax.ShapeDtypeStruct((blk, 128), f32),
        in_specs=[hbm] * 12,
        out_specs=pl.BlockSpec(memory_space=pltpu.VMEM),
        scratch_shapes=[
            pltpu.SMEM(neighbours.shape[::-1], jnp.int32),
            pltpu.SMEM(octant.shape, jnp.int32),
            pltpu.SMEM(octant.shape, jnp.int32),
            pltpu.SMEM(inter_list.shape[::-1], jnp.int32),
            pltpu.SMEM(inter_list.shape[::-1], jnp.int32),
            pltpu.SMEM(inter_list.shape[::-1], jnp.int32),
            pltpu.VMEM((2 * blk, 128), bf16),
            pltpu.VMEM((2 * boxes, 8, 128), f32),
            pltpu.VMEM(near_blocks.shape, bf16),
            pltpu.VMEM(lift.shape, bf16),
            pltpu.VMEM(place.shape, bf16),
            pltpu.VMEM((share, interp.shape[1]), bf16),
            pltpu.VMEM((2 * share, 2 * interp.shape[1]), bf16),
            pltpu.VMEM((8, 2, share), f32),
            pltpu.VMEM(translators.shape, f32),
            pltpu.VMEM((2 * translators.shape[0], 8, 128), f32),
            pltpu.VMEM((blk, 128), f32),
            pltpu.VMEM((boxes, 128), f32),
            pltpu.VMEM((nsamp, blk + boxes, 128), bf16),
            pltpu.VMEM((3 * parents * 8, 128), f32),
            pltpu.VMEM((3 * parents, 8, 128), f32),
            pltpu.VMEM((4, 2, parents, 128), bf16),
            pltpu.VMEM((2, 4, 2, parents, 128), bf16),
            pltpu.VMEM((parents * 8, 128), f32),
            pltpu.VMEM((nz, blk, 128), f32),
            pltpu.VMEM((blk, 128), f32),
            pltpu.VMEM((nz, blk, 128), bf16),
            pltpu.VMEM((nz, blk, 128), bf16),
            pltpu.VMEM((nz, blk, 128), bf16),
            pltpu.VMEM((nz, blk, 128), bf16),
            pltpu.VMEM((nz, blk, 128), bf16),
            pltpu.VMEM((blk, 128), f32),
            pltpu.VMEM((blk, 128), f32),
            dma((boxes,)),
            dma((6,)), dma((5,)),
            dma((2,)), dma((2,)),
            dma((nsamp,)), dma((nsamp,)),
            dma((2, 4)), dma((2, 4)),
            dma((nz, 2)), dma((nz, 2)),
            dma((nz,)), dma((nz,)),
            dma((nz,)), dma((nz,)),
        ],
        compiler_params=pltpu.CompilerParams(
            collective_id=0, has_side_effects=True, vmem_limit_bytes=48 * 1024 * 1024
        ),
    )(
        *[
            pltpu.with_memory_space_constraint(a, pltpu.HBM)
            for a in (
                neighbours.T, octant, leaf_parent_index, inter_list.T, trans_id.T,
                x2, near_blocks, lift, place, interp, phases, translators,
            )
        ]
    )
    return out.reshape(xvec.shape)


def solution(mesh):
    lead = ("box", "samp")
    in_specs = (
        P(lead, None, None, None),
        P(lead, None, None, None, None),
        P(lead, None),
        P(lead, None, None, None),
        P(lead, None, None, None),
        P(),
        P(),
        P(lead),
        P(lead),
        P(None, None, "samp"),
        P("box", None),
        P("box", None),
    )
    return jax.shard_map(
        on_device, mesh=mesh, in_specs=in_specs, out_specs=P(lead, None, None, None), check_vma=False
    )
```

```python
import jax
import jax.numpy as jnp
from jax import lax
from jax.experimental import pallas as pl
from jax.experimental.pallas import tpu as pltpu
from jax.sharding import PartitionSpec as P

f32 = jnp.float32
bf16 = jnp.bfloat16
MESH = pl.DeviceIdType.MESH
NT_DIMS = (((1,), (1,)), ((), ()))


def dot_nt(a, b):
    return lax.dot_general(a, b, NT_DIMS, preferred_element_type=f32)


def dot_nn(a, b):
    return jnp.dot(a, b, preferred_element_type=f32)


def times_i(v):
    swapped = pltpu.roll(v, 4, 0)
    row = lax.broadcasted_iota(jnp.int32, v.shape, 0)
    return jnp.where(row < 4, -swapped, swapped)


def make_kernel(nbox, nsamp, boxes, parents, near_k, list_k, sample_share):
    half = boxes // 2
    total_boxes = boxes * nsamp * nbox
    total_parents = parents * nbox
    blk = boxes * 8
    pb = parents * 8
    slots = boxes * nsamp
    nz = nsamp // 2
    half_rows = blk // 2
    relay_out = (7, 6, 1, 2)
    relay_back = (1, 2, 7, 6)
    share = sample_share

    def kernel(
        nbr_hbm, octs_hbm, pars_hbm, ilist_hbm, tids_hbm,
        x_hbm, near_hbm, lift_hbm, place_hbm, interp_hbm, phases_hbm, trans_hbm,
        out,
        nbr, octs, pars, ilist, tids, wtab,
        xh, xf, nearm, liftm, placem, interpm, twin, phm, trm, trb,
        patf, slotf, gbuf, parf, parw, parb, hbuf, incf,
        ownf, crossf, xsend, xrecv, brecv, zsend, zrecv, nearf, fieldf,
        near_sem, in_sem, idx_sem,
        halo_send, halo_recv, g_send, g_recv, h_send, h_recv,
        ax_send, ax_recv, b_send, b_recv, az_send, az_recv,
    ):
        b = lax.axis_index("box")
        s = lax.axis_index("samp")
        me = b * nsamp + s
        ndev = nbox * nsamp

        x_cp = pltpu.make_async_copy(x_hbm, xh.at[pl.ds(half * 8, blk)], in_sem.at[0])
        lift_cp = pltpu.make_async_copy(lift_hbm, liftm, in_sem.at[1])
        interp_cp = pltpu.make_async_copy(
            interp_hbm.at[pl.ds(pl.multiple_of(s * share, share), share)], interpm, in_sem.at[2]
        )
        ph_cp = pltpu.make_async_copy(
            phases_hbm.at[:, :, pl.ds(pl.multiple_of(s * share, share), share)], phm, in_sem.at[3]
        )
        tr_cp = pltpu.make_async_copy(trans_hbm, trm, in_sem.at[4])
        place_cp = pltpu.make_async_copy(place_hbm, placem, in_sem.at[5])
        near_cps = [
            pltpu.make_async_copy(near_hbm.at[n], nearm.at[n], near_sem.at[n]) for n in range(boxes)
        ]
        idx_cps = [
            pltpu.make_async_copy(src, dst, idx_sem.at[i])
            for i, (src, dst) in enumerate(
                ((octs_hbm, octs), (pars_hbm, pars), (nbr_hbm, nbr), (ilist_hbm, ilist), (tids_hbm, tids))
            )
        ]
        x_cp.start()
        lift_cp.start()
        for cp in idx_cps:
            cp.start()

        barrier = pltpu.get_barrier_semaphore()
        right = lax.rem(me + 1, ndev)
        left = lax.rem(me + ndev - 1, ndev)
        right_id = (right // nsamp, lax.rem(right, nsamp))
        left_id = (left // nsamp, lax.rem(left, nsamp))
        up_id = (lax.rem(b + 1, nbox), s)
        down_id = (lax.rem(b + nbox - 1, nbox), s)

        z, xhi = s // 2, lax.rem(s, 2)
        partner = (b, s + 1 - 2 * xhi)

        def along(t):
            return (b, 2 * lax.rem(z + t + nz, nz) + xhi)

        for dev in (right_id, left_id, up_id, down_id, partner):
            pl.semaphore_signal(barrier, inc=1, device_id=dev, device_id_type=MESH)
        for t in range(1, nz):
            pl.semaphore_signal(barrier, inc=1, device_id=along(t), device_id_type=MESH)

        interp_cp.start()
        ph_cp.start()
        tr_cp.start()
        for cp in near_cps[: boxes // 2]:
            cp.start()
        place_cp.start()
        for cp in near_cps[boxes // 2 :]:
            cp.start()

        idx_cps[0].wait()
        idx_cps[1].wait()
        for n in range(boxes):
            slot = octs[n] * parents + (pars[n] - b * parents)
            slotf[pl.ds(n, 1), :] = jnp.full((1, 128), slot, jnp.int32).astype(f32)
        x_cp.wait()
        xf[pl.ds(half, boxes)] = xh[pl.ds(half * 8, blk), :].astype(f32).reshape(boxes, 8, 128)
        lift_cp.wait()

        for n in range(boxes):
            xn = xf[half + n].astype(bf16)
            o = dot_nt(xn, liftm[n].reshape(2 * liftm.shape[2], liftm.shape[3]))
            patf[pl.ds(n, 8, stride=boxes), :] = o[:, :128] + times_i(o[:, 128:])
        gbuf[0, pl.ds(0, blk), :] = patf[...].astype(bf16)
        gbuf[0, pl.ds(blk, boxes), :] = slotf[...].astype(bf16)

        pl.semaphore_wait(barrier, nz - 1 + 5)

        to_right = pltpu.make_async_remote_copy(
            src_ref=xh.at[pl.ds(blk, half * 8)], dst_ref=xh.at[pl.ds(0, half * 8)],
            send_sem=halo_send.at[0], recv_sem=halo_recv.at[0],
            device_id=right_id, device_id_type=MESH,
        )
        to_left = pltpu.make_async_remote_copy(
            src_ref=xh.at[pl.ds(half * 8, half * 8)], dst_ref=xh.at[pl.ds(blk + half * 8, half * 8)],
            send_sem=halo_send.at[1], recv_sem=halo_recv.at[1],
            device_id=left_id, device_id_type=MESH,
        )
        to_right.start()
        to_left.start()
        order = sorted(range(1, nz), key=lambda t: -min(t, nz - t))

        def spread_out(t):
            return pltpu.make_async_remote_copy(
                src_ref=gbuf.at[0], dst_ref=gbuf.at[t],
                send_sem=g_send.at[t], recv_sem=g_recv.at[t],
                device_id=along(t), device_id_type=MESH,
            )

        def hand_over(t):
            return pltpu.make_async_remote_copy(
                src_ref=gbuf.at[t], dst_ref=gbuf.at[nz + t],
                send_sem=g_send.at[nz + t], recv_sem=g_recv.at[nz + t],
                device_id=partner, device_id_type=MESH,
            )

        def pass_on(t):
            return pltpu.make_async_remote_copy(
                src_ref=gbuf.at[nz], dst_ref=gbuf.at[nz + t],
                send_sem=g_send.at[nz + t], recv_sem=g_recv.at[nz + t],
                device_id=along(t), device_id_type=MESH,
            )

        gathers = {t: spread_out(t) for t in order}
        gathers.update({nz + t: pass_on(t) if t in relay_out else hand_over(t) for t in range(nz)})
        gathers[nz].start()
        for t in order:
            gathers[t].start()

        for cp in idx_cps[2:]:
            cp.wait()

        def window(p, carry):
            for k in range(list_k):
                w = lax.rem(ilist[k, p] - b * parents + parents + total_parents, total_parents)
                wtab[k, p] = jnp.minimum(w, 3 * parents - 1)
            return carry

        lax.fori_loop(0, parents, window, 0)
        to_right.wait()
        to_left.wait()
        xf[pl.ds(0, half)] = xh[pl.ds(0, half * 8), :].astype(f32).reshape(half, 8, 128)
        xf[pl.ds(half + boxes, half)] = (
            xh[pl.ds(blk + half * 8, half * 8), :].astype(f32).reshape(half, 8, 128)
        )

        def near_box(n, carry):
            pltpu.make_async_copy(near_hbm.at[n], nearm.at[n], near_sem.at[n]).wait()
            acc = jnp.zeros((8, 256), f32)
            for k in range(near_k):
                idx = lax.rem(nbr[k, n] - me * boxes + half + total_boxes, 2 * boxes)
                xk = xf[idx].astype(bf16)
                acc = acc + dot_nt(xk, nearm[n, k].reshape(256, 128))
            nearf[pl.ds(pl.multiple_of(n * 8, 8), 8), :] = acc[:, :128] + times_i(acc[:, 128:])
            return carry

        lax.fori_loop(0, 3, near_box, 0)
        gathers[nz].wait_recv()
        for t in relay_out:
            gathers[nz + t].start()
        done = 3
        for i, t in enumerate(order):
            upto = 3 + (boxes // 2 - 3) * (i + 1) // len(order)
            lax.fori_loop(done, upto, near_box, 0)
            done = upto
            gathers[t].wait_recv()
            if t not in relay_out:
                gathers[nz + t].start()

        interp_cp.wait()
        twin[...] = jnp.zeros(twin.shape, bf16)
        twin[pl.ds(0, share), pl.ds(0, 128)] = interpm[...]
        twin[pl.ds(share, share), pl.ds(128, 128)] = interpm[...]
        ph_cp.wait()
        tr_cp.wait()

        def widen(t, carry):
            op = trm[t]
            trb[2 * t] = jnp.broadcast_to(op[0:1], (8, 128))
            trb[2 * t + 1] = jnp.broadcast_to(op[1:2], (8, 128))
            return carry

        lax.fori_loop(0, trm.shape[0], widen, 0, unroll=8)
        for t in order:
            gathers[t].wait_send()
        gathers[nz].wait_send()
        for t in order:
            gathers[nz + t].wait()

        ids = gbuf[:, pl.ds(blk, boxes), :].reshape(slots, 128).astype(f32)
        lane = lax.broadcasted_iota(jnp.int32, (slots, 128), 1).astype(f32)
        spread = jnp.concatenate(
            [jnp.where(ids == lane + 128.0 * h, 1.0, 0.0) for h in range(slots // 128)], axis=1
        ).astype(bf16)
        ids_t = ids.T
        row = lax.broadcasted_iota(jnp.int32, (128, slots), 0).astype(f32)
        gather_m = jnp.concatenate(
            [jnp.where(ids_t == row + 128.0 * h, 1.0, 0.0) for h in range(slots // 128)], axis=0
        ).astype(bf16)

        def raised(r):
            pair = jnp.concatenate(
                [
                    gbuf[:, pl.ds(cr * boxes, boxes), :].reshape(slots, 128)
                    for cr in (r, 4 + r)
                ],
                axis=1,
            )
            return dot_nt(dot_nn(gather_m, pair).astype(bf16), twin[...])

        halos = {
            side: pltpu.make_async_remote_copy(
                src_ref=parb, dst_ref=hbuf.at[side],
                send_sem=h_send.at[side, 0], recv_sem=h_recv.at[side, 0],
                device_id=(up_id, down_id)[side], device_id_type=MESH,
            )
            for side in range(2)
        }
        for r in range(4):
            both = raised(r)
            ar, ai = both[:, :128], both[:, 128:]
            pr = jnp.zeros((parents, 128), f32)
            pi = jnp.zeros((parents, 128), f32)
            for o in range(8):
                fr, fi = phm[o, pl.ds(0, 1), :], phm[o, pl.ds(1, 1), :]
                br, bi = ar[o * parents : (o + 1) * parents], ai[o * parents : (o + 1) * parents]
                pr = pr + (fr * br - fi * bi)
                pi = pi + (fr * bi + fi * br)
            parb[r, 0] = pr.astype(bf16)
            parb[r, 1] = pi.astype(bf16)
            if r == 3:
                for side in range(2):
                    halos[side].start()

        def keep(block, src):
            for r in range(4):
                for c in range(2):
                    parf[pl.ds(block * pb + 4 * c + r, parents, stride=8), :] = src(r, c).astype(f32)
            parw[pl.ds(block * parents, parents)] = parf[pl.ds(block * pb, pb), :].reshape(parents, 8, 128)

        keep(1, lambda r, c: parb[r, c])
        for side in range(2):
            halos[side].wait()
            keep(2 * side, lambda r, c: hbuf[side, r, c])

        def translate(p, carry):
            s1 = jnp.zeros((8, 128), f32)
            s2 = jnp.zeros((8, 128), f32)
            for k in range(list_k):
                v = parw[wtab[k, p]]
                t = 2 * tids[k, p]
                s1 = s1 + trb[t] * v
                s2 = s2 + trb[t + 1] * v
            inc = (s1 + times_i(s2)).astype(bf16).astype(f32)
            incf[pl.ds(pl.multiple_of(p * 8, 8), 8), :] = inc
            return carry

        lax.fori_loop(0, parents, translate, 0, unroll=4)

        turn = [t for t in order if t not in relay_back] + [0]
        to_partner = {
            t: pltpu.make_async_remote_copy(
                src_ref=xsend.at[t], dst_ref=xrecv.at[t],
                send_sem=ax_send.at[t, 0], recv_sem=ax_recv.at[t, 0],
                device_id=partner, device_id_type=MESH,
            )
            for t in turn
        }
        to_relay = {
            t: pltpu.make_async_remote_copy(
                src_ref=xsend.at[t], dst_ref=brecv.at[t],
                send_sem=b_send.at[t], recv_sem=b_recv.at[t],
                device_id=along(-t), device_id_type=MESH,
            )
            for t in relay_back
        }
        to_owner = {
            t: pltpu.make_async_remote_copy(
                src_ref=zsend.at[t], dst_ref=zrecv.at[t],
                send_sem=az_send.at[t], recv_sem=az_recv.at[t],
                device_id=along(-t), device_id_type=MESH,
            )
            for t in range(1, nz)
        }
        rows = slots // 2
        for r in range(4):
            ir = incf[pl.ds(r, parents, stride=8), :]
            ii = incf[pl.ds(4 + r, parents, stride=8), :]
            sr, si = [], []
            for o in range(8):
                fr, fi = phm[o, pl.ds(0, 1), :], phm[o, pl.ds(1, 1), :]
                sr.append((fr * ir - fi * ii).astype(bf16))
                si.append((fr * ii + fi * ir).astype(bf16))
            pair = jnp.concatenate([jnp.concatenate(sr, axis=0), jnp.concatenate(si, axis=0)], axis=1)
            both = dot_nn(dot_nn(spread, pair).astype(bf16), twin[...])
            for cr, low in ((2 * r, both[:, :128]), (2 * r + 1, both[:, 128:])):
                ownf[:, pl.ds(cr * boxes, boxes), :] = low[:rows].reshape(nz, boxes, 128)
                xsend[:, pl.ds(cr * boxes, boxes), :] = low[rows:].astype(bf16).reshape(nz, boxes, 128)
                crossf[pl.ds(cr * boxes, boxes), :] = low[rows : rows + boxes]
            if r == 3:
                for t in turn[:-1]:
                    to_partner[t].start()
        for t in relay_back:
            to_relay[t].start()
        for t in relay_back:
            zsend[t] = ownf[t].astype(bf16)
            to_owner[t].start()

        def add_partner(t):
            to_partner[t].wait_recv()
            zsend[t] = (ownf[t] + xrecv[t].astype(f32)).astype(bf16)
            to_owner[t].start()

        add_partner(turn[0])
        cross = crossf[...]
        for t in relay_back:
            to_relay[t].wait_recv()
            cross = cross + brecv[t].astype(f32)
        xsend[0] = cross.astype(bf16)
        to_partner[0].start()
        for t in turn[1:-1]:
            add_partner(t)
        lax.fori_loop(boxes // 2, boxes, near_box, 0)
        to_partner[0].wait_recv()
        field = ownf[0] + xrecv[0].astype(f32)
        for t in turn:
            to_partner[t].wait_send()
        for t in relay_back:
            to_relay[t].wait_send()
        for t in order[::-1]:
            to_owner[t].wait()
            field = field + zrecv[t].astype(f32)
        for r in range(4):
            for c in range(2):
                fieldf[pl.ds((4 * c + r) * boxes, boxes), :] = (
                    field[(2 * r + c) * boxes : (2 * r + c + 1) * boxes]
                )
        place_cp.wait()
        for n in range(boxes):
            fn = fieldf[pl.ds(n, 8, stride=boxes), :].astype(bf16)
            o = dot_nt(fn, placem[n].reshape(256, 128))
            out[pl.ds(n * 8, 8), :] = nearf[pl.ds(n * 8, 8), :] + o[:, :128] + times_i(o[:, 128:])

    return kernel


def on_device(
    xvec, near_blocks, neighbours, lift, place, interp, phases, octant,
    leaf_parent_index, translators, inter_list, trans_id,
):
    boxes = xvec.shape[0]
    nsamp = lax.axis_size("samp")
    nbox = lax.axis_size("box")
    parents = inter_list.shape[0]
    share = interp.shape[0] // nsamp
    blk = boxes * 8
    nz = nsamp // 2
    x2 = xvec.reshape(blk, 128)
    hbm = pl.BlockSpec(memory_space=pltpu.HBM)
    dma = pltpu.SemaphoreType.DMA
    out = pl.pallas_call(
        make_kernel(nbox, nsamp, boxes, parents, neighbours.shape[1], inter_list.shape[1], share),
        out_shape=jax.ShapeDtypeStruct((blk, 128), f32),
        in_specs=[hbm] * 12,
        out_specs=pl.BlockSpec(memory_space=pltpu.VMEM),
        scratch_shapes=[
            pltpu.SMEM(neighbours.shape[::-1], jnp.int32),
            pltpu.SMEM(octant.shape, jnp.int32),
            pltpu.SMEM(octant.shape, jnp.int32),
            pltpu.SMEM(inter_list.shape[::-1], jnp.int32),
            pltpu.SMEM(inter_list.shape[::-1], jnp.int32),
            pltpu.SMEM(inter_list.shape[::-1], jnp.int32),
            pltpu.VMEM((2 * blk, 128), bf16),
            pltpu.VMEM((2 * boxes, 8, 128), f32),
            pltpu.VMEM(near_blocks.shape, bf16),
            pltpu.VMEM(lift.shape, bf16),
            pltpu.VMEM(place.shape, bf16),
            pltpu.VMEM((share, interp.shape[1]), bf16),
            pltpu.VMEM((2 * share, 2 * interp.shape[1]), bf16),
            pltpu.VMEM((8, 2, share), f32),
            pltpu.VMEM(translators.shape, f32),
            pltpu.VMEM((2 * translators.shape[0], 8, 128), f32),
            pltpu.VMEM((blk, 128), f32),
            pltpu.VMEM((boxes, 128), f32),
            pltpu.VMEM((nsamp, blk + boxes, 128), bf16),
            pltpu.VMEM((3 * parents * 8, 128), f32),
            pltpu.VMEM((3 * parents, 8, 128), f32),
            pltpu.VMEM((4, 2, parents, 128), bf16),
            pltpu.VMEM((2, 4, 2, parents, 128), bf16),
            pltpu.VMEM((parents * 8, 128), f32),
            pltpu.VMEM((nz, blk, 128), f32),
            pltpu.VMEM((blk, 128), f32),
            pltpu.VMEM((nz, blk, 128), bf16),
            pltpu.VMEM((nz, blk, 128), bf16),
            pltpu.VMEM((nz, blk, 128), bf16),
            pltpu.VMEM((nz, blk, 128), bf16),
            pltpu.VMEM((nz, blk, 128), bf16),
            pltpu.VMEM((blk, 128), f32),
            pltpu.VMEM((blk, 128), f32),
            dma((boxes,)),
            dma((6,)), dma((5,)),
            dma((2,)), dma((2,)),
            dma((nsamp,)), dma((nsamp,)),
            dma((2, 4)), dma((2, 4)),
            dma((nz, 2)), dma((nz, 2)),
            dma((nz,)), dma((nz,)),
            dma((nz,)), dma((nz,)),
        ],
        compiler_params=pltpu.CompilerParams(
            collective_id=0, has_side_effects=True, vmem_limit_bytes=48 * 1024 * 1024
        ),
    )(
        *[
            pltpu.with_memory_space_constraint(a, pltpu.HBM)
            for a in (
                neighbours.T, octant, leaf_parent_index, inter_list.T, trans_id.T,
                x2, near_blocks, lift, place, interp, phases, translators,
            )
        ]
    )
    return out.reshape(xvec.shape)


def solution(mesh):
    lead = ("box", "samp")
    in_specs = (
        P(lead, None, None, None),
        P(lead, None, None, None, None),
        P(lead, None),
        P(lead, None, None, None),
        P(lead, None, None, None),
        P(),
        P(),
        P(lead),
        P(lead),
        P(None, None, "samp"),
        P("box", None),
        P("box", None),
    )
    return jax.shard_map(
        on_device, mesh=mesh, in_specs=in_specs, out_specs=P(lead, None, None, None), check_vma=False
    )
```

```python
import jax
import jax.numpy as jnp
from jax import lax
from jax.experimental import pallas as pl
from jax.experimental.pallas import tpu as pltpu
from jax.sharding import PartitionSpec as P

f32 = jnp.float32
bf16 = jnp.bfloat16
MESH = pl.DeviceIdType.MESH
NT_DIMS = (((1,), (1,)), ((), ()))


def dot_nt(a, b):
    return lax.dot_general(a, b, NT_DIMS, preferred_element_type=f32)


def dot_nn(a, b):
    return jnp.dot(a, b, preferred_element_type=f32)


def times_i(v):
    swapped = pltpu.roll(v, 4, 0)
    row = lax.broadcasted_iota(jnp.int32, v.shape, 0)
    return jnp.where(row < 4, -swapped, swapped)


def make_kernel(nbox, nsamp, boxes, parents, near_k, list_k, sample_share):
    half = boxes // 2
    total_boxes = boxes * nsamp * nbox
    total_parents = parents * nbox
    blk = boxes * 8
    pb = parents * 8
    slots = boxes * nsamp
    nz = nsamp // 2
    half_rows = blk // 2
    relay_out = (7, 6, 1, 2)
    relay_back = (1, 2, 7, 6)
    share = sample_share

    def kernel(
        nbr_hbm, octs_hbm, pars_hbm, ilist_hbm, tids_hbm,
        x_hbm, near_hbm, lift_hbm, place_hbm, interp_hbm, phases_hbm, trans_hbm,
        out,
        nbr, octs, pars, ilist, tids, wtab,
        xh, xf, nearm, liftm, placem, interpm, twin, phm, trm, trb,
        patf, slotf, gbuf, parf, parw, parb, hbuf, incf,
        ownf, crossf, xsend, xrecv, brecv, zsend, zrecv, nearf, fieldf,
        near_sem, in_sem, idx_sem,
        halo_send, halo_recv, g_send, g_recv, h_send, h_recv,
        ax_send, ax_recv, b_send, b_recv, az_send, az_recv,
    ):
        b = lax.axis_index("box")
        s = lax.axis_index("samp")
        me = b * nsamp + s
        ndev = nbox * nsamp

        x_cp = pltpu.make_async_copy(x_hbm, xh.at[pl.ds(half * 8, blk)], in_sem.at[0])
        lift_cp = pltpu.make_async_copy(lift_hbm, liftm, in_sem.at[1])
        interp_cp = pltpu.make_async_copy(
            interp_hbm.at[pl.ds(pl.multiple_of(s * share, share), share)], interpm, in_sem.at[2]
        )
        ph_cp = pltpu.make_async_copy(
            phases_hbm.at[:, :, pl.ds(pl.multiple_of(s * share, share), share)], phm, in_sem.at[3]
        )
        tr_cp = pltpu.make_async_copy(trans_hbm, trm, in_sem.at[4])
        place_cp = pltpu.make_async_copy(place_hbm, placem, in_sem.at[5])
        near_cps = [
            pltpu.make_async_copy(near_hbm.at[n], nearm.at[n], near_sem.at[n]) for n in range(boxes)
        ]
        idx_cps = [
            pltpu.make_async_copy(src, dst, idx_sem.at[i])
            for i, (src, dst) in enumerate(
                ((octs_hbm, octs), (pars_hbm, pars), (nbr_hbm, nbr), (ilist_hbm, ilist), (tids_hbm, tids))
            )
        ]
        x_cp.start()
        lift_cp.start()
        for cp in idx_cps:
            cp.start()

        barrier = pltpu.get_barrier_semaphore()
        right = lax.rem(me + 1, ndev)
        left = lax.rem(me + ndev - 1, ndev)
        right_id = (right // nsamp, lax.rem(right, nsamp))
        left_id = (left // nsamp, lax.rem(left, nsamp))
        up_id = (lax.rem(b + 1, nbox), s)
        down_id = (lax.rem(b + nbox - 1, nbox), s)

        z, xhi = s // 2, lax.rem(s, 2)
        partner = (b, s + 1 - 2 * xhi)

        def along(t):
            return (b, 2 * lax.rem(z + t + nz, nz) + xhi)

        for dev in (right_id, left_id, up_id, down_id, partner):
            pl.semaphore_signal(barrier, inc=1, device_id=dev, device_id_type=MESH)
        for t in range(1, nz):
            pl.semaphore_signal(barrier, inc=1, device_id=along(t), device_id_type=MESH)

        interp_cp.start()
        ph_cp.start()
        tr_cp.start()
        for cp in near_cps[: boxes // 2]:
            cp.start()
        place_cp.start()
        for cp in near_cps[boxes // 2 :]:
            cp.start()

        idx_cps[0].wait()
        idx_cps[1].wait()
        for n in range(boxes):
            slot = octs[n] * parents + (pars[n] - b * parents)
            slotf[pl.ds(n, 1), :] = jnp.full((1, 128), slot, jnp.int32).astype(f32)
        x_cp.wait()
        xf[pl.ds(half, boxes)] = xh[pl.ds(half * 8, blk), :].astype(f32).reshape(boxes, 8, 128)
        lift_cp.wait()

        for n in range(boxes):
            xn = xf[half + n].astype(bf16)
            o = dot_nt(xn, liftm[n].reshape(2 * liftm.shape[2], liftm.shape[3]))
            patf[pl.ds(n, 8, stride=boxes), :] = o[:, :128] + times_i(o[:, 128:])
        gbuf[0, pl.ds(0, blk), :] = patf[...].astype(bf16)
        gbuf[0, pl.ds(blk, boxes), :] = slotf[...].astype(bf16)

        pl.semaphore_wait(barrier, nz - 1 + 5)

        to_right = pltpu.make_async_remote_copy(
            src_ref=xh.at[pl.ds(blk, half * 8)], dst_ref=xh.at[pl.ds(0, half * 8)],
            send_sem=halo_send.at[0], recv_sem=halo_recv.at[0],
            device_id=right_id, device_id_type=MESH,
        )
        to_left = pltpu.make_async_remote_copy(
            src_ref=xh.at[pl.ds(half * 8, half * 8)], dst_ref=xh.at[pl.ds(blk + half * 8, half * 8)],
            send_sem=halo_send.at[1], recv_sem=halo_recv.at[1],
            device_id=left_id, device_id_type=MESH,
        )
        to_right.start()
        to_left.start()
        order = sorted(range(1, nz), key=lambda t: -min(t, nz - t))

        def spread_out(t):
            return pltpu.make_async_remote_copy(
                src_ref=gbuf.at[0], dst_ref=gbuf.at[t],
                send_sem=g_send.at[t], recv_sem=g_recv.at[t],
                device_id=along(t), device_id_type=MESH,
            )

        def hand_over(t):
            return pltpu.make_async_remote_copy(
                src_ref=gbuf.at[t], dst_ref=gbuf.at[nz + t],
                send_sem=g_send.at[nz + t], recv_sem=g_recv.at[nz + t],
                device_id=partner, device_id_type=MESH,
            )

        def pass_on(t):
            return pltpu.make_async_remote_copy(
                src_ref=gbuf.at[nz], dst_ref=gbuf.at[nz + t],
                send_sem=g_send.at[nz + t], recv_sem=g_recv.at[nz + t],
                device_id=along(t), device_id_type=MESH,
            )

        gathers = {t: spread_out(t) for t in order}
        gathers.update({nz + t: pass_on(t) if t in relay_out else hand_over(t) for t in range(nz)})
        gathers[nz].start()
        for t in order:
            gathers[t].start()

        for cp in idx_cps[2:]:
            cp.wait()

        def window(p, carry):
            for k in range(list_k):
                w = lax.rem(ilist[k, p] - b * parents + parents + total_parents, total_parents)
                wtab[k, p] = jnp.minimum(w, 3 * parents - 1)
            return carry

        lax.fori_loop(0, parents, window, 0)
        to_right.wait()
        to_left.wait()
        xf[pl.ds(0, half)] = xh[pl.ds(0, half * 8), :].astype(f32).reshape(half, 8, 128)
        xf[pl.ds(half + boxes, half)] = (
            xh[pl.ds(blk + half * 8, half * 8), :].astype(f32).reshape(half, 8, 128)
        )

        def near_box(n, carry):
            pltpu.make_async_copy(near_hbm.at[n], nearm.at[n], near_sem.at[n]).wait()
            acc = jnp.zeros((8, 256), f32)
            for k in range(near_k):
                idx = lax.rem(nbr[k, n] - me * boxes + half + total_boxes, 2 * boxes)
                xk = xf[idx].astype(bf16)
                acc = acc + dot_nt(xk, nearm[n, k].reshape(256, 128))
            nearf[pl.ds(pl.multiple_of(n * 8, 8), 8), :] = acc[:, :128] + times_i(acc[:, 128:])
            return carry

        lax.fori_loop(0, 3, near_box, 0)
        gathers[nz].wait_recv()
        for t in relay_out:
            gathers[nz + t].start()
        done = 3
        for i, t in enumerate(order):
            upto = 3 + (boxes // 2 - 3) * (i + 1) // len(order)
            lax.fori_loop(done, upto, near_box, 0)
            done = upto
            gathers[t].wait_recv()
            if t not in relay_out:
                gathers[nz + t].start()

        interp_cp.wait()
        twin[...] = jnp.zeros(twin.shape, bf16)
        twin[pl.ds(0, share), pl.ds(0, 128)] = interpm[...]
        twin[pl.ds(share, share), pl.ds(128, 128)] = interpm[...]
        ph_cp.wait()
        tr_cp.wait()

        def widen(t, carry):
            op = trm[t]
            trb[2 * t] = jnp.broadcast_to(op[0:1], (8, 128))
            trb[2 * t + 1] = jnp.broadcast_to(op[1:2], (8, 128))
            return carry

        lax.fori_loop(0, trm.shape[0], widen, 0, unroll=8)
        for t in order:
            gathers[t].wait_send()
        gathers[nz].wait_send()
        for t in order:
            gathers[nz + t].wait()

        ids = gbuf[:, pl.ds(blk, boxes), :].reshape(slots, 128).astype(f32)
        lane = lax.broadcasted_iota(jnp.int32, (slots, 128), 1).astype(f32)
        spread = jnp.concatenate(
            [jnp.where(ids == lane + 128.0 * h, 1.0, 0.0) for h in range(slots // 128)], axis=1
        ).astype(bf16)
        ids_t = ids.T
        row = lax.broadcasted_iota(jnp.int32, (128, slots), 0).astype(f32)
        gather_m = jnp.concatenate(
            [jnp.where(ids_t == row + 128.0 * h, 1.0, 0.0) for h in range(slots // 128)], axis=0
        ).astype(bf16)

        def raised(r):
            pair = jnp.concatenate(
                [
                    gbuf[:, pl.ds(cr * boxes, boxes), :].reshape(slots, 128)
                    for cr in (r, 4 + r)
                ],
                axis=1,
            )
            return dot_nt(dot_nn(gather_m, pair).astype(bf16), twin[...])

        halos = {
            side: pltpu.make_async_remote_copy(
                src_ref=parb, dst_ref=hbuf.at[side],
                send_sem=h_send.at[side, 0], recv_sem=h_recv.at[side, 0],
                device_id=(up_id, down_id)[side], device_id_type=MESH,
            )
            for side in range(2)
        }
        for r in range(4):
            both = raised(r)
            ar, ai = both[:, :128], both[:, 128:]
            pr = jnp.zeros((parents, 128), f32)
            pi = jnp.zeros((parents, 128), f32)
            for o in range(8):
                fr, fi = phm[o, pl.ds(0, 1), :], phm[o, pl.ds(1, 1), :]
                br, bi = ar[o * parents : (o + 1) * parents], ai[o * parents : (o + 1) * parents]
                pr = pr + (fr * br - fi * bi)
                pi = pi + (fr * bi + fi * br)
            parb[r, 0] = pr.astype(bf16)
            parb[r, 1] = pi.astype(bf16)
            if r == 3:
                for side in range(2):
                    halos[side].start()

        def keep(block, src):
            for r in range(4):
                for c in range(2):
                    parf[pl.ds(block * pb + 4 * c + r, parents, stride=8), :] = src(r, c).astype(f32)
            parw[pl.ds(block * parents, parents)] = parf[pl.ds(block * pb, pb), :].reshape(parents, 8, 128)

        keep(1, lambda r, c: parb[r, c])
        for side in range(2):
            halos[side].wait()
            keep(2 * side, lambda r, c: hbuf[side, r, c])

        def translate(p, carry):
            s1 = jnp.zeros((8, 128), f32)
            s2 = jnp.zeros((8, 128), f32)
            for k in range(list_k):
                v = parw[wtab[k, p]]
                t = 2 * tids[k, p]
                s1 = s1 + trb[t] * v
                s2 = s2 + trb[t + 1] * v
            inc = (s1 + times_i(s2)).astype(bf16).astype(f32)
            incf[pl.ds(pl.multiple_of(p * 8, 8), 8), :] = inc
            return carry

        lax.fori_loop(0, parents, translate, 0, unroll=8)

        turn = [t for t in order if t not in relay_back] + [0]
        to_partner = {
            t: pltpu.make_async_remote_copy(
                src_ref=xsend.at[t], dst_ref=xrecv.at[t],
                send_sem=ax_send.at[t, 0], recv_sem=ax_recv.at[t, 0],
                device_id=partner, device_id_type=MESH,
            )
            for t in turn
        }
        to_relay = {
            t: pltpu.make_async_remote_copy(
                src_ref=xsend.at[t], dst_ref=brecv.at[t],
                send_sem=b_send.at[t], recv_sem=b_recv.at[t],
                device_id=along(-t), device_id_type=MESH,
            )
            for t in relay_back
        }
        to_owner = {
            t: pltpu.make_async_remote_copy(
                src_ref=zsend.at[t], dst_ref=zrecv.at[t],
                send_sem=az_send.at[t], recv_sem=az_recv.at[t],
                device_id=along(-t), device_id_type=MESH,
            )
            for t in range(1, nz)
        }
        rows = slots // 2
        for r in range(4):
            ir = incf[pl.ds(r, parents, stride=8), :]
            ii = incf[pl.ds(4 + r, parents, stride=8), :]
            sr, si = [], []
            for o in range(8):
                fr, fi = phm[o, pl.ds(0, 1), :], phm[o, pl.ds(1, 1), :]
                sr.append((fr * ir - fi * ii).astype(bf16))
                si.append((fr * ii + fi * ir).astype(bf16))
            pair = jnp.concatenate([jnp.concatenate(sr, axis=0), jnp.concatenate(si, axis=0)], axis=1)
            both = dot_nn(dot_nn(spread, pair).astype(bf16), twin[...])
            for cr, low in ((2 * r, both[:, :128]), (2 * r + 1, both[:, 128:])):
                ownf[:, pl.ds(cr * boxes, boxes), :] = low[:rows].reshape(nz, boxes, 128)
                xsend[:, pl.ds(cr * boxes, boxes), :] = low[rows:].astype(bf16).reshape(nz, boxes, 128)
                crossf[pl.ds(cr * boxes, boxes), :] = low[rows : rows + boxes]
        for t in relay_back:
            to_relay[t].start()
        for t in turn[:-1]:
            to_partner[t].start()
        for t in relay_back:
            zsend[t] = ownf[t].astype(bf16)
            to_owner[t].start()

        def add_partner(t):
            to_partner[t].wait_recv()
            zsend[t] = (ownf[t] + xrecv[t].astype(f32)).astype(bf16)
            to_owner[t].start()

        cross = crossf[...]
        for t in relay_back:
            to_relay[t].wait_recv()
            cross = cross + brecv[t].astype(f32)
        xsend[0] = cross.astype(bf16)
        to_partner[0].start()
        for t in turn[:-1]:
            add_partner(t)
        lax.fori_loop(boxes // 2, boxes, near_box, 0)
        to_partner[0].wait_recv()
        field = ownf[0] + xrecv[0].astype(f32)
        for t in turn:
            to_partner[t].wait_send()
        for t in relay_back:
            to_relay[t].wait_send()
        for t in order[::-1]:
            to_owner[t].wait()
            field = field + zrecv[t].astype(f32)
        for r in range(4):
            for c in range(2):
                fieldf[pl.ds((4 * c + r) * boxes, boxes), :] = (
                    field[(2 * r + c) * boxes : (2 * r + c + 1) * boxes]
                )
        place_cp.wait()
        for n in range(boxes):
            fn = fieldf[pl.ds(n, 8, stride=boxes), :].astype(bf16)
            o = dot_nt(fn, placem[n].reshape(256, 128))
            out[pl.ds(n * 8, 8), :] = nearf[pl.ds(n * 8, 8), :] + o[:, :128] + times_i(o[:, 128:])

    return kernel


def on_device(
    xvec, near_blocks, neighbours, lift, place, interp, phases, octant,
    leaf_parent_index, translators, inter_list, trans_id,
):
    boxes = xvec.shape[0]
    nsamp = lax.axis_size("samp")
    nbox = lax.axis_size("box")
    parents = inter_list.shape[0]
    share = interp.shape[0] // nsamp
    blk = boxes * 8
    nz = nsamp // 2
    x2 = xvec.reshape(blk, 128)
    hbm = pl.BlockSpec(memory_space=pltpu.HBM)
    dma = pltpu.SemaphoreType.DMA
    out = pl.pallas_call(
        make_kernel(nbox, nsamp, boxes, parents, neighbours.shape[1], inter_list.shape[1], share),
        out_shape=jax.ShapeDtypeStruct((blk, 128), f32),
        in_specs=[hbm] * 12,
        out_specs=pl.BlockSpec(memory_space=pltpu.VMEM),
        scratch_shapes=[
            pltpu.SMEM(neighbours.shape[::-1], jnp.int32),
            pltpu.SMEM(octant.shape, jnp.int32),
            pltpu.SMEM(octant.shape, jnp.int32),
            pltpu.SMEM(inter_list.shape[::-1], jnp.int32),
            pltpu.SMEM(inter_list.shape[::-1], jnp.int32),
            pltpu.SMEM(inter_list.shape[::-1], jnp.int32),
            pltpu.VMEM((2 * blk, 128), bf16),
            pltpu.VMEM((2 * boxes, 8, 128), f32),
            pltpu.VMEM(near_blocks.shape, bf16),
            pltpu.VMEM(lift.shape, bf16),
            pltpu.VMEM(place.shape, bf16),
            pltpu.VMEM((share, interp.shape[1]), bf16),
            pltpu.VMEM((2 * share, 2 * interp.shape[1]), bf16),
            pltpu.VMEM((8, 2, share), f32),
            pltpu.VMEM(translators.shape, f32),
            pltpu.VMEM((2 * translators.shape[0], 8, 128), f32),
            pltpu.VMEM((blk, 128), f32),
            pltpu.VMEM((boxes, 128), f32),
            pltpu.VMEM((nsamp, blk + boxes, 128), bf16),
            pltpu.VMEM((3 * parents * 8, 128), f32),
            pltpu.VMEM((3 * parents, 8, 128), f32),
            pltpu.VMEM((4, 2, parents, 128), bf16),
            pltpu.VMEM((2, 4, 2, parents, 128), bf16),
            pltpu.VMEM((parents * 8, 128), f32),
            pltpu.VMEM((nz, blk, 128), f32),
            pltpu.VMEM((blk, 128), f32),
            pltpu.VMEM((nz, blk, 128), bf16),
            pltpu.VMEM((nz, blk, 128), bf16),
            pltpu.VMEM((nz, blk, 128), bf16),
            pltpu.VMEM((nz, blk, 128), bf16),
            pltpu.VMEM((nz, blk, 128), bf16),
            pltpu.VMEM((blk, 128), f32),
            pltpu.VMEM((blk, 128), f32),
            dma((boxes,)),
            dma((6,)), dma((5,)),
            dma((2,)), dma((2,)),
            dma((nsamp,)), dma((nsamp,)),
            dma((2, 4)), dma((2, 4)),
            dma((nz, 2)), dma((nz, 2)),
            dma((nz,)), dma((nz,)),
            dma((nz,)), dma((nz,)),
        ],
        compiler_params=pltpu.CompilerParams(
            collective_id=0, has_side_effects=True, vmem_limit_bytes=48 * 1024 * 1024
        ),
    )(
        *[
            pltpu.with_memory_space_constraint(a, pltpu.HBM)
            for a in (
                neighbours.T, octant, leaf_parent_index, inter_list.T, trans_id.T,
                x2, near_blocks, lift, place, interp, phases, translators,
            )
        ]
    )
    return out.reshape(xvec.shape)


def solution(mesh):
    lead = ("box", "samp")
    in_specs = (
        P(lead, None, None, None),
        P(lead, None, None, None, None),
        P(lead, None),
        P(lead, None, None, None),
        P(lead, None, None, None),
        P(),
        P(),
        P(lead),
        P(lead),
        P(None, None, "samp"),
        P("box", None),
        P("box", None),
    )
    return jax.shard_map(
        on_device, mesh=mesh, in_specs=in_specs, out_specs=P(lead, None, None, None), check_vma=False
    )
```

```python
import jax
import jax.numpy as jnp
from jax import lax
from jax.experimental import pallas as pl
from jax.experimental.pallas import tpu as pltpu
from jax.sharding import PartitionSpec as P

f32 = jnp.float32
bf16 = jnp.bfloat16
MESH = pl.DeviceIdType.MESH
NT_DIMS = (((1,), (1,)), ((), ()))


def dot_nt(a, b):
    return lax.dot_general(a, b, NT_DIMS, preferred_element_type=f32)


def dot_nn(a, b):
    return jnp.dot(a, b, preferred_element_type=f32)


def times_i(v):
    swapped = pltpu.roll(v, 4, 0)
    row = lax.broadcasted_iota(jnp.int32, v.shape, 0)
    return jnp.where(row < 4, -swapped, swapped)


def make_kernel(nbox, nsamp, boxes, parents, near_k, list_k, sample_share):
    half = boxes // 2
    total_boxes = boxes * nsamp * nbox
    total_parents = parents * nbox
    blk = boxes * 8
    pb = parents * 8
    slots = boxes * nsamp
    nz = nsamp // 2
    half_rows = blk // 2
    relay_out = (7, 6, 1, 2)
    relay_back = (1, 2, 7, 6)
    share = sample_share

    def kernel(
        nbr_hbm, octs_hbm, pars_hbm, ilist_hbm, tids_hbm,
        x_hbm, near_hbm, lift_hbm, place_hbm, interp_hbm, phases_hbm, trans_hbm,
        out,
        nbr, octs, pars, ilist, tids, wtab,
        xh, xf, nearm, liftm, placem, interpm, twin, phm, trm, trb,
        patf, slotf, gbuf, parf, parw, parb, hbuf, incf,
        ownf, crossf, xsend, xrecv, brecv, zsend, zrecv, nearf, fieldf,
        near_sem, in_sem, idx_sem,
        halo_send, halo_recv, g_send, g_recv, h_send, h_recv,
        ax_send, ax_recv, b_send, b_recv, az_send, az_recv,
    ):
        b = lax.axis_index("box")
        s = lax.axis_index("samp")
        me = b * nsamp + s
        ndev = nbox * nsamp

        x_cp = pltpu.make_async_copy(x_hbm, xh.at[pl.ds(half * 8, blk)], in_sem.at[0])
        lift_cp = pltpu.make_async_copy(lift_hbm, liftm, in_sem.at[1])
        interp_cp = pltpu.make_async_copy(
            interp_hbm.at[pl.ds(pl.multiple_of(s * share, share), share)], interpm, in_sem.at[2]
        )
        ph_cp = pltpu.make_async_copy(
            phases_hbm.at[:, :, pl.ds(pl.multiple_of(s * share, share), share)], phm, in_sem.at[3]
        )
        tr_cp = pltpu.make_async_copy(trans_hbm, trm, in_sem.at[4])
        place_cp = pltpu.make_async_copy(place_hbm, placem, in_sem.at[5])
        near_cps = [
            pltpu.make_async_copy(near_hbm.at[n], nearm.at[n], near_sem.at[n]) for n in range(boxes)
        ]
        idx_cps = [
            pltpu.make_async_copy(src, dst, idx_sem.at[i])
            for i, (src, dst) in enumerate(
                ((octs_hbm, octs), (pars_hbm, pars), (nbr_hbm, nbr), (ilist_hbm, ilist), (tids_hbm, tids))
            )
        ]
        x_cp.start()
        lift_cp.start()
        for cp in idx_cps:
            cp.start()

        barrier = pltpu.get_barrier_semaphore()
        right = lax.rem(me + 1, ndev)
        left = lax.rem(me + ndev - 1, ndev)
        right_id = (right // nsamp, lax.rem(right, nsamp))
        left_id = (left // nsamp, lax.rem(left, nsamp))
        up_id = (lax.rem(b + 1, nbox), s)
        down_id = (lax.rem(b + nbox - 1, nbox), s)

        z, xhi = s // 2, lax.rem(s, 2)
        partner = (b, s + 1 - 2 * xhi)

        def along(t):
            return (b, 2 * lax.rem(z + t + nz, nz) + xhi)

        for dev in (right_id, left_id, up_id, down_id, partner):
            pl.semaphore_signal(barrier, inc=1, device_id=dev, device_id_type=MESH)
        for t in range(1, nz):
            pl.semaphore_signal(barrier, inc=1, device_id=along(t), device_id_type=MESH)

        interp_cp.start()
        ph_cp.start()
        tr_cp.start()
        for cp in near_cps[: boxes // 2]:
            cp.start()
        place_cp.start()
        for cp in near_cps[boxes // 2 :]:
            cp.start()

        idx_cps[0].wait()
        idx_cps[1].wait()
        for n in range(boxes):
            slot = octs[n] * parents + (pars[n] - b * parents)
            slotf[pl.ds(n, 1), :] = jnp.full((1, 128), slot, jnp.int32).astype(f32)
        x_cp.wait()
        xf[pl.ds(half, boxes)] = xh[pl.ds(half * 8, blk), :].astype(f32).reshape(boxes, 8, 128)
        lift_cp.wait()

        for n in range(boxes):
            xn = xf[half + n].astype(bf16)
            o = dot_nt(xn, liftm[n].reshape(2 * liftm.shape[2], liftm.shape[3]))
            patf[pl.ds(n, 8, stride=boxes), :] = o[:, :128] + times_i(o[:, 128:])
        gbuf[0, pl.ds(0, blk), :] = patf[...].astype(bf16)
        gbuf[0, pl.ds(blk, boxes), :] = slotf[...].astype(bf16)

        pl.semaphore_wait(barrier, nz - 1 + 5)

        to_right = pltpu.make_async_remote_copy(
            src_ref=xh.at[pl.ds(blk, half * 8)], dst_ref=xh.at[pl.ds(0, half * 8)],
            send_sem=halo_send.at[0], recv_sem=halo_recv.at[0],
            device_id=right_id, device_id_type=MESH,
        )
        to_left = pltpu.make_async_remote_copy(
            src_ref=xh.at[pl.ds(half * 8, half * 8)], dst_ref=xh.at[pl.ds(blk + half * 8, half * 8)],
            send_sem=halo_send.at[1], recv_sem=halo_recv.at[1],
            device_id=left_id, device_id_type=MESH,
        )
        to_right.start()
        to_left.start()
        order = sorted(range(1, nz), key=lambda t: -min(t, nz - t))

        def spread_out(t):
            return pltpu.make_async_remote_copy(
                src_ref=gbuf.at[0], dst_ref=gbuf.at[t],
                send_sem=g_send.at[t], recv_sem=g_recv.at[t],
                device_id=along(t), device_id_type=MESH,
            )

        def hand_over(t):
            return pltpu.make_async_remote_copy(
                src_ref=gbuf.at[t], dst_ref=gbuf.at[nz + t],
                send_sem=g_send.at[nz + t], recv_sem=g_recv.at[nz + t],
                device_id=partner, device_id_type=MESH,
            )

        def pass_on(t):
            return pltpu.make_async_remote_copy(
                src_ref=gbuf.at[nz], dst_ref=gbuf.at[nz + t],
                send_sem=g_send.at[nz + t], recv_sem=g_recv.at[nz + t],
                device_id=along(t), device_id_type=MESH,
            )

        gathers = {t: spread_out(t) for t in order}
        gathers.update({nz + t: pass_on(t) if t in relay_out else hand_over(t) for t in range(nz)})
        gathers[nz].start()
        for t in order:
            gathers[t].start()

        for cp in idx_cps[2:]:
            cp.wait()

        def window(p, carry):
            for k in range(list_k):
                w = lax.rem(ilist[k, p] - b * parents + parents + total_parents, total_parents)
                wtab[k, p] = jnp.minimum(w, 3 * parents - 1)
            return carry

        lax.fori_loop(0, parents, window, 0)
        to_right.wait()
        to_left.wait()
        xf[pl.ds(0, half)] = xh[pl.ds(0, half * 8), :].astype(f32).reshape(half, 8, 128)
        xf[pl.ds(half + boxes, half)] = (
            xh[pl.ds(blk + half * 8, half * 8), :].astype(f32).reshape(half, 8, 128)
        )

        def near_box(n, carry):
            pltpu.make_async_copy(near_hbm.at[n], nearm.at[n], near_sem.at[n]).wait()
            acc = jnp.zeros((8, 256), f32)
            for k in range(near_k):
                idx = lax.rem(nbr[k, n] - me * boxes + half + total_boxes, 2 * boxes)
                xk = xf[idx].astype(bf16)
                acc = acc + dot_nt(xk, nearm[n, k].reshape(256, 128))
            nearf[pl.ds(pl.multiple_of(n * 8, 8), 8), :] = acc[:, :128] + times_i(acc[:, 128:])
            return carry

        lax.fori_loop(0, 3, near_box, 0)
        gathers[nz].wait_recv()
        for t in relay_out:
            gathers[nz + t].start()
        done = 3
        for i, t in enumerate(order):
            upto = 3 + (boxes // 2 - 3) * (i + 1) // len(order)
            lax.fori_loop(done, upto, near_box, 0)
            done = upto
            gathers[t].wait_recv()
            if t not in relay_out:
                gathers[nz + t].start()

        interp_cp.wait()
        twin[...] = jnp.zeros(twin.shape, bf16)
        twin[pl.ds(0, share), pl.ds(0, 128)] = interpm[...]
        twin[pl.ds(share, share), pl.ds(128, 128)] = interpm[...]
        ph_cp.wait()
        tr_cp.wait()

        def widen(t, carry):
            op = trm[t]
            trb[2 * t] = jnp.broadcast_to(op[0:1], (8, 128))
            trb[2 * t + 1] = jnp.broadcast_to(op[1:2], (8, 128))
            return carry

        lax.fori_loop(0, trm.shape[0], widen, 0, unroll=8)
        for t in order:
            gathers[t].wait_send()
        gathers[nz].wait_send()
        for t in order:
            gathers[nz + t].wait()

        ids = gbuf[:, pl.ds(blk, boxes), :].reshape(slots, 128).astype(f32)
        ids_t = ids.T
        row = lax.broadcasted_iota(jnp.int32, (128, slots), 0).astype(f32)
        gather_m = jnp.concatenate(
            [jnp.where(ids_t == row + 128.0 * h, 1.0, 0.0) for h in range(slots // 128)], axis=0
        ).astype(bf16)

        def raised(r):
            pair = jnp.concatenate(
                [
                    gbuf[:, pl.ds(cr * boxes, boxes), :].reshape(slots, 128)
                    for cr in (r, 4 + r)
                ],
                axis=1,
            )
            return dot_nt(dot_nn(gather_m, pair).astype(bf16), twin[...])

        halos = {
            side: pltpu.make_async_remote_copy(
                src_ref=parb, dst_ref=hbuf.at[side],
                send_sem=h_send.at[side, 0], recv_sem=h_recv.at[side, 0],
                device_id=(up_id, down_id)[side], device_id_type=MESH,
            )
            for side in range(2)
        }
        for r in range(4):
            both = raised(r)
            ar, ai = both[:, :128], both[:, 128:]
            pr = jnp.zeros((parents, 128), f32)
            pi = jnp.zeros((parents, 128), f32)
            for o in range(8):
                fr, fi = phm[o, pl.ds(0, 1), :], phm[o, pl.ds(1, 1), :]
                br, bi = ar[o * parents : (o + 1) * parents], ai[o * parents : (o + 1) * parents]
                pr = pr + (fr * br - fi * bi)
                pi = pi + (fr * bi + fi * br)
            parb[r, 0] = pr.astype(bf16)
            parb[r, 1] = pi.astype(bf16)
            if r == 3:
                for side in range(2):
                    halos[side].start()

        def keep(block, src):
            for r in range(4):
                for c in range(2):
                    parf[pl.ds(block * pb + 4 * c + r, parents, stride=8), :] = src(r, c).astype(f32)
            parw[pl.ds(block * parents, parents)] = parf[pl.ds(block * pb, pb), :].reshape(parents, 8, 128)

        lane = lax.broadcasted_iota(jnp.int32, (slots, 128), 1).astype(f32)
        spread = jnp.concatenate(
            [jnp.where(ids == lane + 128.0 * h, 1.0, 0.0) for h in range(slots // 128)], axis=1
        ).astype(bf16)
        keep(1, lambda r, c: parb[r, c])
        for side in range(2):
            halos[side].wait()
            keep(2 * side, lambda r, c: hbuf[side, r, c])

        def translate(p, carry):
            s1 = jnp.zeros((8, 128), f32)
            s2 = jnp.zeros((8, 128), f32)
            for k in range(list_k):
                v = parw[wtab[k, p]]
                t = 2 * tids[k, p]
                s1 = s1 + trb[t] * v
                s2 = s2 + trb[t + 1] * v
            inc = (s1 + times_i(s2)).astype(bf16).astype(f32)
            incf[pl.ds(pl.multiple_of(p * 8, 8), 8), :] = inc
            return carry

        lax.fori_loop(0, parents, translate, 0, unroll=4)

        turn = [t for t in order if t not in relay_back] + [0]
        to_partner = {
            t: pltpu.make_async_remote_copy(
                src_ref=xsend.at[t], dst_ref=xrecv.at[t],
                send_sem=ax_send.at[t, 0], recv_sem=ax_recv.at[t, 0],
                device_id=partner, device_id_type=MESH,
            )
            for t in turn
        }
        to_relay = {
            t: pltpu.make_async_remote_copy(
                src_ref=xsend.at[t], dst_ref=brecv.at[t],
                send_sem=b_send.at[t], recv_sem=b_recv.at[t],
                device_id=along(-t), device_id_type=MESH,
            )
            for t in relay_back
        }
        to_owner = {
            t: pltpu.make_async_remote_copy(
                src_ref=zsend.at[t], dst_ref=zrecv.at[t],
                send_sem=az_send.at[t], recv_sem=az_recv.at[t],
                device_id=along(-t), device_id_type=MESH,
            )
            for t in range(1, nz)
        }
        rows = slots // 2
        for r in range(4):
            ir = incf[pl.ds(r, parents, stride=8), :]
            ii = incf[pl.ds(4 + r, parents, stride=8), :]
            sr, si = [], []
            for o in range(8):
                fr, fi = phm[o, pl.ds(0, 1), :], phm[o, pl.ds(1, 1), :]
                sr.append((fr * ir - fi * ii).astype(bf16))
                si.append((fr * ii + fi * ir).astype(bf16))
            pair = jnp.concatenate([jnp.concatenate(sr, axis=0), jnp.concatenate(si, axis=0)], axis=1)
            both = dot_nn(dot_nn(spread, pair).astype(bf16), twin[...])
            for cr, low in ((2 * r, both[:, :128]), (2 * r + 1, both[:, 128:])):
                ownf[:, pl.ds(cr * boxes, boxes), :] = low[:rows].reshape(nz, boxes, 128)
                xsend[:, pl.ds(cr * boxes, boxes), :] = low[rows:].astype(bf16).reshape(nz, boxes, 128)
                crossf[pl.ds(cr * boxes, boxes), :] = low[rows : rows + boxes]
            if r == 3:
                for t in turn[:-1]:
                    to_partner[t].start()
        for t in relay_back:
            to_relay[t].start()
        for t in relay_back:
            zsend[t] = ownf[t].astype(bf16)
            to_owner[t].start()

        def add_partner(t):
            to_partner[t].wait_recv()
            zsend[t] = (ownf[t] + xrecv[t].astype(f32)).astype(bf16)
            to_owner[t].start()

        add_partner(turn[0])
        cross = crossf[...]
        for t in relay_back:
            to_relay[t].wait_recv()
            cross = cross + brecv[t].astype(f32)
        xsend[0] = cross.astype(bf16)
        to_partner[0].start()
        for t in turn[1:-1]:
            add_partner(t)
        lax.fori_loop(boxes // 2, boxes, near_box, 0)
        to_partner[0].wait_recv()
        field = ownf[0] + xrecv[0].astype(f32)
        for t in turn:
            to_partner[t].wait_send()
        for t in relay_back:
            to_relay[t].wait_send()
        for t in order[::-1]:
            to_owner[t].wait()
            field = field + zrecv[t].astype(f32)
        for r in range(4):
            for c in range(2):
                fieldf[pl.ds((4 * c + r) * boxes, boxes), :] = (
                    field[(2 * r + c) * boxes : (2 * r + c + 1) * boxes]
                )
        place_cp.wait()
        for n in range(boxes):
            fn = fieldf[pl.ds(n, 8, stride=boxes), :].astype(bf16)
            o = dot_nt(fn, placem[n].reshape(256, 128))
            out[pl.ds(n * 8, 8), :] = nearf[pl.ds(n * 8, 8), :] + o[:, :128] + times_i(o[:, 128:])

    return kernel


def on_device(
    xvec, near_blocks, neighbours, lift, place, interp, phases, octant,
    leaf_parent_index, translators, inter_list, trans_id,
):
    boxes = xvec.shape[0]
    nsamp = lax.axis_size("samp")
    nbox = lax.axis_size("box")
    parents = inter_list.shape[0]
    share = interp.shape[0] // nsamp
    blk = boxes * 8
    nz = nsamp // 2
    x2 = xvec.reshape(blk, 128)
    hbm = pl.BlockSpec(memory_space=pltpu.HBM)
    dma = pltpu.SemaphoreType.DMA
    out = pl.pallas_call(
        make_kernel(nbox, nsamp, boxes, parents, neighbours.shape[1], inter_list.shape[1], share),
        out_shape=jax.ShapeDtypeStruct((blk, 128), f32),
        in_specs=[hbm] * 12,
        out_specs=pl.BlockSpec(memory_space=pltpu.VMEM),
        scratch_shapes=[
            pltpu.SMEM(neighbours.shape[::-1], jnp.int32),
            pltpu.SMEM(octant.shape, jnp.int32),
            pltpu.SMEM(octant.shape, jnp.int32),
            pltpu.SMEM(inter_list.shape[::-1], jnp.int32),
            pltpu.SMEM(inter_list.shape[::-1], jnp.int32),
            pltpu.SMEM(inter_list.shape[::-1], jnp.int32),
            pltpu.VMEM((2 * blk, 128), bf16),
            pltpu.VMEM((2 * boxes, 8, 128), f32),
            pltpu.VMEM(near_blocks.shape, bf16),
            pltpu.VMEM(lift.shape, bf16),
            pltpu.VMEM(place.shape, bf16),
            pltpu.VMEM((share, interp.shape[1]), bf16),
            pltpu.VMEM((2 * share, 2 * interp.shape[1]), bf16),
            pltpu.VMEM((8, 2, share), f32),
            pltpu.VMEM(translators.shape, f32),
            pltpu.VMEM((2 * translators.shape[0], 8, 128), f32),
            pltpu.VMEM((blk, 128), f32),
            pltpu.VMEM((boxes, 128), f32),
            pltpu.VMEM((nsamp, blk + boxes, 128), bf16),
            pltpu.VMEM((3 * parents * 8, 128), f32),
            pltpu.VMEM((3 * parents, 8, 128), f32),
            pltpu.VMEM((4, 2, parents, 128), bf16),
            pltpu.VMEM((2, 4, 2, parents, 128), bf16),
            pltpu.VMEM((parents * 8, 128), f32),
            pltpu.VMEM((nz, blk, 128), f32),
            pltpu.VMEM((blk, 128), f32),
            pltpu.VMEM((nz, blk, 128), bf16),
            pltpu.VMEM((nz, blk, 128), bf16),
            pltpu.VMEM((nz, blk, 128), bf16),
            pltpu.VMEM((nz, blk, 128), bf16),
            pltpu.VMEM((nz, blk, 128), bf16),
            pltpu.VMEM((blk, 128), f32),
            pltpu.VMEM((blk, 128), f32),
            dma((boxes,)),
            dma((6,)), dma((5,)),
            dma((2,)), dma((2,)),
            dma((nsamp,)), dma((nsamp,)),
            dma((2, 4)), dma((2, 4)),
            dma((nz, 2)), dma((nz, 2)),
            dma((nz,)), dma((nz,)),
            dma((nz,)), dma((nz,)),
        ],
        compiler_params=pltpu.CompilerParams(
            collective_id=0, has_side_effects=True, vmem_limit_bytes=48 * 1024 * 1024
        ),
    )(
        *[
            pltpu.with_memory_space_constraint(a, pltpu.HBM)
            for a in (
                neighbours.T, octant, leaf_parent_index, inter_list.T, trans_id.T,
                x2, near_blocks, lift, place, interp, phases, translators,
            )
        ]
    )
    return out.reshape(xvec.shape)


def solution(mesh):
    lead = ("box", "samp")
    in_specs = (
        P(lead, None, None, None),
        P(lead, None, None, None, None),
        P(lead, None),
        P(lead, None, None, None),
        P(lead, None, None, None),
        P(),
        P(),
        P(lead),
        P(lead),
        P(None, None, "samp"),
        P("box", None),
        P("box", None),
    )
    return jax.shard_map(
        on_device, mesh=mesh, in_specs=in_specs, out_specs=P(lead, None, None, None), check_vma=False
    )
```
